768 devices in a mesh: pw: 16 (over y, core), band: 48 (over x, z).
Axes of the slice: x: 4, y: 8, z: 12, core: 2. Of those that a mesh axis runs over, the one named last changes fastest.
Arguments:
- psi: bfloat16 [2, 48, 98304], P(None, 'band', 'pw'), may hold values from -9 to 9
- gvec_index: int32 [98304], P('pw'), may hold values from 0 to 442367, as said below
- vloc: float32 [192, 192, 192], P(None, 'pw'), may hold values from -3 to 1
- beta: bfloat16 [2, 72, 98304], P(None, None, 'pw'), may hold values from -0.078125 to 0.078125
- dmat: float32 [4, 18, 18], replicated, may hold values from -1 to 3
- qmat: float32 [4, 18, 18], replicated, may hold values from -1 to 2
Outputs:
- hpsi: bfloat16 [2, 48, 98304], P(None, 'band', 'pw')
- spsi: bfloat16 [2, 48, 98304], P(None, 'band', 'pw')
- gram: float32 [2, 48, 48], P(None, 'band')
The draws below stay inside these ranges and needn't reach their ends.
Inputs may be any that keep to these rules, and one draw needn't show every extreme that they name: `gvec_index`: each entry is (x - k * 12) * 192 * 192 + y * 192 + z for the grid cell (x, y, z) of its plane wave, where k is the entry's block of 6144 plane waves and x lies in k * 12 .. (k + 1) * 12 - 1; no cell appears twice.
All inputs are finite; a program needn't handle non-finite values.
Results may differ from the reference program's by a relative error of at most 0.0069.
Values may be sent and summed in bfloat16 or wider, within the bound.
A program may use at most 64 MiB of HBM per device.

```python
import jax
import jax.numpy as jnp
from jax import lax

NG = 192
PROJ_ATOM = 18
ATOMS = 4
PW_DEV = 6144
PW = 98304
BANDS = 48
NPROJ = 72
N_PW = 16


def draw_psi(key, part):
    folded_key = jax.random.fold_in(key, 101)
    subkeys = jax.random.split(folded_key, 5)
    samples = jnp.clip(jax.random.normal(subkeys[0], (2, BANDS, PW), jnp.float32), -4.0, 4.0)
    first_order = jax.random.permutation(subkeys[1], BANDS)
    second_order = jax.random.permutation(subkeys[2], BANDS)
    first_weight = jax.random.uniform(subkeys[3], (BANDS,), jnp.float32, 0.3, 0.6)
    second_weight = jax.random.uniform(subkeys[4], (BANDS,), jnp.float32, 0.3, 0.6)
    blended = samples + first_weight[None, :, None] * samples[:, first_order] + second_weight[None, :, None] * samples[:, second_order]
    return blended.astype(jnp.bfloat16)


def draw_gvec_index(key, part):
    folded_key = jax.random.fold_in(key, 202)
    slab_cells = NG // N_PW * NG * NG

    def one_block(position):
        block_key = jax.random.fold_in(folded_key, position)
        inner = jax.random.permutation(jax.random.fold_in(block_key, 1), slab_cells - 2)[:PW_DEV - 2] + 1
        ends = jnp.array([0, slab_cells - 1], dtype=jnp.int32)
        full = jnp.concatenate([ends, inner.astype(jnp.int32)])
        order = jax.random.permutation(jax.random.fold_in(block_key, 2), PW_DEV)
        return full[order]
    blocks = jax.vmap(one_block)(jnp.arange(N_PW, dtype=jnp.int32))
    return blocks.reshape(-1).astype(jnp.int32)


def block_matrix(key, salt, lowest, highest, spread):
    subkeys = jax.random.split(jax.random.fold_in(key, salt), 2)
    diagonal = jax.random.uniform(subkeys[0], (ATOMS, PROJ_ATOM), jnp.float32, lowest, highest)
    coupling = jax.random.normal(subkeys[1], (ATOMS, PROJ_ATOM, PROJ_ATOM), jnp.float32) * spread
    coupling = 0.5 * (coupling + jnp.swapaxes(coupling, 1, 2))
    identity = jnp.eye(PROJ_ATOM, dtype=jnp.float32)
    return coupling * (1.0 - identity)[None] + diagonal[:, :, None] * identity[None]


def draw_dmat(key, part):
    return block_matrix(key, 303, 1.5, 3.0, 0.15)


def draw_qmat(key, part):
    return block_matrix(key, 404, 0.8, 1.6, 0.08)


def shard_levels(key, extent, cuts, smallest, high):
    def one(axis_at, parts):
        steps = jax.random.uniform(jax.random.fold_in(jax.random.fold_in(key, 6), axis_at), (parts,), jnp.float32, smallest / len(cuts), high / len(cuts))
        return jnp.repeat(jnp.exp(steps), extent[axis_at] // parts).reshape((-1,) + (1,) * (len(extent) - axis_at - 1))

    level = one(*cuts[0])
    for cut in cuts[1:]:
        level = level * one(*cut)
    return level


def normal_values(rng, shape, deviation, bound, cuts=(), kind=jnp.bfloat16):
    entries = jax.random.normal(rng, shape, jnp.float32) * deviation
    if len(cuts) > 0:
        entries = shard_levels(rng, shape, cuts, -0.22, 0.18) * entries
    return jnp.clip(entries, min=-bound, max=bound).astype(kind)


def setup_inputs(seed: int = 0) -> dict:
    seeds = jax.random.split(jax.random.key(seed), 7)
    psi = draw_psi(jax.random.fold_in(seeds[6], 71), 0)
    gvec_index = draw_gvec_index(jax.random.fold_in(seeds[6], 71), 0)
    vloc = jnp.clip(-3.0 + 4.0 * jax.random.uniform(seeds[2], (NG, NG, NG), jnp.float32) ** shard_levels(seeds[2], (NG, NG, NG), ((1, 16),), -0.2, 0.2), -3.0, 1.0)
    beta = normal_values(seeds[3], (2, NPROJ, PW), (PW_DEV * N_PW // 16) ** -0.5, 0.078125, ((2, 16),))
    dmat = draw_dmat(jax.random.fold_in(seeds[6], 71), 0)
    qmat = draw_qmat(jax.random.fold_in(seeds[6], 71), 0)
    return dict(psi=psi, gvec_index=gvec_index, vloc=vloc, beta=beta, dmat=dmat, qmat=qmat)


def dft_table(length, orient):
    counter = jnp.arange(length, dtype=jnp.int32)
    phase = counter[:, None] * counter[None, :] % length
    angle = phase.astype(jnp.float32) * (2.0 * jnp.pi / length)
    factor = 1.0 / jnp.sqrt(jnp.float32(length))
    cosine = jnp.cos(angle) * factor
    sine_part = orient * jnp.sin(angle) * factor
    upper = jnp.concatenate([cosine, sine_part], axis=1)
    lower = jnp.concatenate([-sine_part, cosine], axis=1)
    return jnp.concatenate([upper, lower], axis=0).astype(jnp.bfloat16)

def along_last(lattice, matrix):
    return jnp.dot(lattice.astype(jnp.float32), matrix.astype(jnp.float32), precision=lax.Precision.HIGHEST)

def along_middle(lattice, matrix):
    size_a, size_b, size_c = lattice.shape
    halfway = size_c // 2
    shaped = lattice.reshape(size_a, size_b, 2, halfway).astype(jnp.float32)
    square = matrix.reshape(2, halfway, 2, halfway).astype(jnp.float32)
    result = jnp.einsum('xypz,pyqk->xkqz', shaped, square, precision=lax.Precision.HIGHEST)
    return result.reshape(size_a, size_b, size_c)

def along_first(lattice, matrix):
    size_a, size_b, size_c = lattice.shape
    halfway = size_c // 2
    shaped = lattice.reshape(size_a, size_b, 2, halfway).astype(jnp.float32)
    square = matrix.reshape(2, halfway, 2, halfway).astype(jnp.float32)
    result = jnp.einsum('xypz,pxqk->kyqz', shaped, square, precision=lax.Precision.HIGHEST)
    return result.reshape(size_a, size_b, size_c)

def folded(level):
    return jnp.where(level < NG // 2, level, level - NG).astype(jnp.float32)

def pair_dot(left, right):
    return jnp.dot(left, right.T, preferred_element_type=jnp.float32)

def plain_dot(left, right):
    return jnp.dot(left, right, preferred_element_type=jnp.float32)

def reference(psi, gvec_index, vloc, beta, dmat, qmat):
    slab_cells = NG // N_PW * NG * NG
    owner = jnp.arange(PW, dtype=jnp.int32) // PW_DEV
    global_cell = (gvec_index + owner * slab_cells).astype(jnp.int32)
    row_index = global_cell // NG
    column = global_cell % NG
    place_re = (row_index * (2 * NG) + column).astype(jnp.int32)
    place_im = (place_re + NG).astype(jnp.int32)
    plus_table = dft_table(NG, 1.0)
    minus_table = dft_table(NG, -1.0)
    potential = vloc.astype(jnp.float32)[:, :, None, :]

    def local_term(coefs):
        lattice = jnp.zeros((NG * NG * 2 * NG,), jnp.bfloat16)
        lattice = lattice.at[place_re].set(coefs[0]).at[place_im].set(coefs[1])
        lattice = lattice.reshape(NG, NG, 2 * NG)
        lattice = along_last(lattice, plus_table).astype(jnp.bfloat16)
        lattice = along_middle(lattice, plus_table).astype(jnp.bfloat16)
        spatial = along_first(lattice, plus_table).reshape(NG, NG, 2, NG)
        lattice = (spatial * potential).reshape(NG, NG, 2 * NG).astype(jnp.bfloat16)
        lattice = along_first(lattice, minus_table).astype(jnp.bfloat16)
        lattice = along_middle(lattice, minus_table).astype(jnp.bfloat16)
        flat_out = along_last(lattice, minus_table).reshape(-1)
        return jnp.stack([flat_out[place_re], flat_out[place_im]])
    local = lax.map(local_term, jnp.transpose(psi, (1, 0, 2)))
    local = jnp.transpose(local, (1, 0, 2))
    plane_x = folded(global_cell // (NG * NG))
    plane_y = folded(global_cell // NG % NG)
    plane_z = folded(global_cell % NG)
    kinetic = 4.0 * (plane_x * plane_x + plane_y * plane_y + plane_z * plane_z) / (NG * NG)
    proj_re = pair_dot(psi[0], beta[0]) + pair_dot(psi[1], beta[1])
    proj_im = pair_dot(psi[1], beta[0]) - pair_dot(psi[0], beta[1])
    coef = jnp.stack([proj_re, proj_im]).reshape(2, BANDS, ATOMS, PROJ_ATOM)
    d_coef = jnp.einsum('aij,cbaj->cbai', dmat, coef, precision=lax.Precision.HIGHEST)
    d_coef = d_coef.reshape(2, BANDS, NPROJ).astype(jnp.bfloat16)
    q_coef = jnp.einsum('aij,cbaj->cbai', qmat, coef, precision=lax.Precision.HIGHEST)
    q_coef = q_coef.reshape(2, BANDS, NPROJ).astype(jnp.bfloat16)

    def expand(weights):
        real_part = plain_dot(weights[0], beta[0]) - plain_dot(weights[1], beta[1])
        imag_part = plain_dot(weights[0], beta[1]) + plain_dot(weights[1], beta[0])
        return jnp.stack([real_part, imag_part])
    psi_wide = psi.astype(jnp.float32)
    hpsi = (local + kinetic[None, None, :] * psi_wide + expand(d_coef)).astype(jnp.bfloat16)
    spsi = (psi_wide + expand(q_coef)).astype(jnp.bfloat16)
    gram_re = (pair_dot(psi[0], spsi[0]) + pair_dot(psi[1], spsi[1])) / PW
    gram_im = (pair_dot(psi[0], spsi[1]) - pair_dot(psi[1], spsi[0])) / PW
    return (hpsi, spsi, jnp.stack([gram_re, gram_im]))
```

```python
import numpy as np
import jax, jax.numpy as jnp
from jax import lax
from jax.experimental import pallas as pl
from jax.experimental.pallas import tpu as pltpu
from jax.sharding import PartitionSpec as P

NG = 192
KD = 12
F32, BF16 = jnp.float32, jnp.bfloat16
TWO_PI = 2.0 * np.pi
CH = 24
CHB = 16


def dft_tables():
    j = np.arange(NG)
    ang = (j[:, None] * j[None, :] % NG).astype(np.float32) * np.float32(TWO_PI / NG)
    fac = np.float32(1.0) / np.sqrt(np.float32(NG))
    c = np.cos(ang).astype(np.float32) * fac
    s = np.sin(ang).astype(np.float32) * fac
    def zt(sign):
        t = np.zeros((512, 512), np.float32)
        t[:NG, :NG] = c; t[256:256 + NG, 256:256 + NG] = c
        t[:NG, 256:256 + NG] = sign * s; t[256:256 + NG, :NG] = -sign * s
        return t
    pad = (np.arange(NG) // KD) * 16 + np.arange(NG) % KD
    def xt(sign):
        t = np.zeros((2 * NG, 512), np.float32)
        t[:NG, pad] = c; t[NG:, 256 + pad] = c
        t[:NG, 256 + pad] = -sign * s; t[NG:, pad] = sign * s
        return t
    b = lambda t: np.asarray(t, dtype=jnp.bfloat16)
    return b(zt(1.0)), b(zt(-1.0)), b(xt(1.0)), b(xt(1.0).T)


def mod_floor(v, m):
    return v - m * jnp.floor((v + 0.5) * (1.0 / m))


def turn(t):
    h = t * np.float32(np.pi)
    q = h * h
    s = h * (1.0 + q * (-1 / 6 + q * (1 / 120 + q * (-1 / 5040 + q * (1 / 362880 + q * (-1 / 39916800))))))
    c = 1.0 + q * (-1 / 2 + q * (1 / 24 + q * (-1 / 720 + q * (1 / 40320 + q * (-1 / 3628800 + q * (1 / 479001600))))))
    return 1.0 - 2.0 * s * s, 2.0 * s * c


def split_index(idx):
    v = idx.astype(F32)
    x = jnp.floor((v + 0.5) * (1.0 / (NG * NG)))
    r = v - x * (NG * NG)
    y = jnp.floor((r + 0.5) * (1.0 / NG))
    return x, y, r - y * NG


def phases(y, p):
    fac = np.float32(1.0) / np.sqrt(np.float32(NG))
    m = mod_floor(y * p.astype(F32), 16.0)
    ar, ai = turn(jnp.where(m > 8.0, m - 16.0, m) * (1.0 / 16.0))
    wr, wi = turn(jnp.where(y > 96.0, y - 192.0, y) * np.float32(1.0 / NG))
    out = []
    for j in range(KD):
        out.append(((ar * fac).astype(BF16).astype(F32), (ai * fac).astype(BF16).astype(F32)))
        if j < KD - 1:
            ar, ai = ar * wr - ai * wi, ar * wi + ai * wr
    return out


def prep_index(idx, p, li_ref):
    x, y, z = split_index(idx)
    w = x * NG + z
    hi = jnp.floor((w + 0.5) * (1.0 / 256.0))
    li_ref[:, 0, :] = w - hi * 256.0
    li_ref[:, 1, :] = hi
    return phases(y, p)


def one_hot(li_ref, t, n):
    rows = lax.broadcasted_iota(jnp.int32, (256, 128), 0).astype(F32).astype(BF16)
    parts = []
    for k in range(n):
        lo = li_ref[t + k, 0:1, :].astype(BF16)
        parts.append(jnp.where(rows == lo, jnp.array(1, BF16), jnp.array(0, BF16)))
    return jnp.concatenate(parts, axis=1) if n > 1 else parts[0]


def spread(v_ref, li_ref, t, n):
    upper = (lax.broadcasted_iota(jnp.int32, (48, 128), 0) >= 24).astype(F32)
    cols = []
    for k in range(n):
        v = v_ref[t + k]
        v = jnp.concatenate([v, v], axis=0).astype(BF16)
        h = (li_ref[t + k, 1:2, :] - upper).astype(BF16)
        zero = jnp.zeros_like(v)
        rows = [jnp.where(h == jnp.array(2 * q, BF16), v, zero) for q in range(4)]
        rows.append(jnp.where(h == jnp.array(8, BF16), v, zero)[:24])
        cols.append(jnp.concatenate(rows, axis=0))
    return jnp.concatenate(cols, axis=1) if n > 1 else cols[0]


def forward_block(psi, idx, p, base, f_ref, v_ref, li_ref, acc_ref, ch):
    e = prep_index(idx, p, li_ref)
    pr, pi = psi[0].astype(F32), psi[1].astype(F32)
    for j in range(KD):
        er, ei = e[j]
        v_ref[:, j, :] = pr * er - pi * ei
        v_ref[:, KD + j, :] = pr * ei + pi * er
    acc_ref[...] = jnp.zeros_like(acc_ref)

    def step(i, carry):
        t = i * ch
        zt = one_hot(li_ref, t, ch)
        l = spread(v_ref, li_ref, t, ch)
        acc_ref[...] += lax.dot_general(l, zt, (((1,), (1,)), ((), ())), preferred_element_type=F32)
        return carry
    lax.fori_loop(0, 48 // ch, step, 0)
    left = lax.broadcasted_iota(jnp.int32, (24, 128), 1) < 64
    for g in range(3):
        a = [[acc_ref[(3 * g + h) * 24:(3 * g + h + 1) * 24, 128 * q:128 * (q + 1)] for q in range(2)] for h in range(3)]
        r01, r10 = pltpu.roll(a[0][1], 64, 1), pltpu.roll(a[1][0], 64, 1)
        r20, r21 = pltpu.roll(a[2][0], 64, 1), pltpu.roll(a[2][1], 64, 1)
        pieces = [(a[0][0], a[0][1]), (jnp.where(left, r01, r10), r10), (a[1][1], a[2][0]), (jnp.where(left, r20, r21), r21)]
        for k, (low, high) in enumerate(pieces):
            f_ref[base, :, 4 * g + k, 0:128] = low
            f_ref[base, :, 4 * g + k, 128:256] = high
    f_ref[base, :, KD:16, :] = jnp.zeros((24, 16 - KD, 256), F32)


def dense_plane(j, f_ref, vloc_ref, zp, zm, xp, xm):
    dot = lambda a, b: jnp.dot(a, b, preferred_element_type=F32)
    fr, fi = (f_ref[:, c * KD + j].reshape(256, 256).astype(BF16) for c in range(2))
    y = dot(jnp.concatenate([fr, fi], axis=1), zp[...]).astype(BF16)
    y = jnp.concatenate([y[:, 0:NG], y[:, 256:256 + NG]], axis=0)
    s = dot(xp[...], y)
    v = vloc_ref[j]
    s = jnp.concatenate([s[:NG] * v, s[NG:] * v], axis=0).astype(BF16)
    s = dot(xm[...], s).astype(BF16)
    out = dot(s[:256], zm[0:NG, :]) + dot(s[256:], zm[256:256 + NG, :])
    f_ref[:, j] = out[:, :256].reshape(16, 16, 256)
    f_ref[:, KD + j] = out[:, 256:].reshape(16, 16, 256)


def backward_block(idx, p, base, f_ref, e_ref, li_ref, b_ref, s_ref, ch):
    e = prep_index(idx, p, li_ref)
    for j in range(KD):
        er, ei = e[j]
        e_ref[:, j, :] = er
        e_ref[:, KD + j, :] = ei
        e_ref[:, 2 * KD + j, :] = -ei
        e_ref[:, 3 * KD + j, :] = er
    left = lax.broadcasted_iota(jnp.int32, (24, 128), 1) < 64
    for g in range(3):
        x = []
        for k in range(4):
            x.append([f_ref[base, :, 4 * g + k, 128 * q:128 * (q + 1)] for q in range(2)])
        r10, r11 = pltpu.roll(x[1][0], 64, 1), pltpu.roll(x[1][1], 64, 1)
        r30, r31 = pltpu.roll(x[3][0], 64, 1), pltpu.roll(x[3][1], 64, 1)
        pieces = [(x[0][0], jnp.where(left, x[0][1], r10)), (jnp.where(left, r10, r11), x[2][0]),
                  (jnp.where(left, x[2][1], r30), jnp.where(left, r30, r31))]
        for h, (low, high) in enumerate(pieces):
            r = (3 * g + h) * 24
            b_ref[r:r + 24, 0:128] = low
            b_ref[r:r + 24, 128:256] = high

    bm = b_ref[...].astype(BF16)

    def step(i, carry):
        t = i * ch
        tt = jnp.dot(bm, one_hot(li_ref, t, ch), preferred_element_type=F32)
        for k in range(ch):
            hi = jnp.broadcast_to(li_ref[t + k, 1:2, :], (24, 128))
            sel = tt[0:24, 128 * k:128 * (k + 1)]
            for h in range(1, 9):
                sel = jnp.where(hi == float(h), tt[24 * h:24 * (h + 1), 128 * k:128 * (k + 1)], sel)
            ev = e_ref[t + k]
            a, b = sel * ev[:24], sel * ev[24:]
            s_ref[0, t + k] = a[0:8] + a[8:16] + a[16:24]
            s_ref[1, t + k] = b[0:8] + b[8:16] + b[16:24]
        return carry
    lax.fori_loop(0, 48 // ch, step, 0)
    re, im = s_ref[0, :, 0, :], s_ref[1, :, 0, :]
    for k in range(1, 8):
        re = re + s_ref[0, :, k, :]
        im = im + s_ref[1, :, k, :]
    return re, im


N_BAND = 48
N_PW = 16


def pw_peer(p, s):
    k = lax.div(s, 2)
    dy = lax.div(k + 1, 2) * (2 * lax.rem(k, 2) - 1)
    y = lax.rem(lax.div(p, 2) + dy + 8, 8)
    return 2 * y + lax.rem(p + s, 2)


def kernel(psi_ref, idx_ref, vloc_ref, beta_ref, bd_ref, zp, zm, xp, xm, h_ref, s_out, g_out,
           f_ref, v_ref, li_ref, acc_ref, e_ref, b_ref, s_ref, nl_ref, loc_ref, pr_ref,
           ag_psi, ag_idx, pj_send, pj_recv, cf, gb, m_ref, rb, q_send, qb, gs, gr, ls, lr,
           agp_s, agp_r, agi_s, agi_r, pj_s, pj_r, gb_s, gb_r, rb_s, rb_r, q_s, q_r, gr_s, gr_r, ls_s, lr_r):
    p, b = lax.axis_index("pw"), lax.axis_index("band")

    def band_peer(s):
        return lax.rem(b + s, N_BAND)

    def copy_pw(src, dst, ssem, rsem, peer, slot):
        return pltpu.make_async_remote_copy(src_ref=src, dst_ref=dst.at[slot], send_sem=ssem.at[peer],
                                            recv_sem=rsem.at[slot], device_id={"pw": peer},
                                            device_id_type=pl.DeviceIdType.MESH)

    def copy_band(src, dst, ssem, rsem, peer, slot):
        return pltpu.make_async_remote_copy(src_ref=src, dst_ref=dst.at[slot], send_sem=ssem.at[peer],
                                            recv_sem=rsem.at[slot], device_id={"band": peer},
                                            device_id_type=pl.DeviceIdType.MESH)

    def each(first, last, body):
        def step(s, carry):
            body(s)
            return carry
        lax.fori_loop(first, last, step, 0)

    barrier = pltpu.get_barrier_semaphore()
    each(1, N_PW, lambda s: pl.semaphore_signal(barrier, inc=1, device_id={"pw": pw_peer(p, s)},
                                                device_id_type=pl.DeviceIdType.MESH))
    each(1, N_BAND, lambda s: pl.semaphore_signal(barrier, inc=1, device_id={"band": band_peer(s)},
                                                  device_id_type=pl.DeviceIdType.MESH))

    for t in range(48):
        cf[t] = psi_ref[:, 128 * t:128 * (t + 1)].astype(F32)
    ag_psi[p, 0] = cf[:, 0, :].astype(BF16)
    ag_psi[p, 1] = cf[:, 1, :].astype(BF16)
    ag_idx[p] = idx_ref[...]
    gb[b] = cf[b]
    nt = lambda u, w, **k: lax.dot_general(u, w, (((1,), (1,)), ((), ())), preferred_element_type=F32, **k)
    rows = psi_ref[...]
    pr, pi = nt(rows, beta_ref[0]), nt(rows, beta_ref[1])
    pj_send[...] = jnp.zeros_like(pj_send)
    pj_send[0:1, 0:72] = pr[0:1] + pi[1:2]
    pj_send[1:2, 0:72] = pr[1:2] - pi[0:1]
    pj_recv[p] = pj_send[...]
    m_ref[...] = jnp.zeros_like(m_ref)
    pl.semaphore_wait(barrier, N_PW + N_BAND - 2)

    agp = lambda peer, slot: copy_pw(ag_psi.at[p], ag_psi, agp_s, agp_r, peer, slot)
    agi = lambda peer, slot: copy_pw(ag_idx.at[p], ag_idx, agi_s, agi_r, peer, slot)
    pjc = lambda peer, slot: copy_pw(pj_send, pj_recv, pj_s, pj_r, peer, slot)
    gbc = lambda peer, slot: copy_band(cf.at[peer], gb, gb_s, gb_r, peer, slot)
    rbc = lambda peer, slot: copy_band(m_ref.at[peer], rb, rb_s, rb_r, peer, slot)
    qbc = lambda peer, slot: copy_band(q_send, qb, q_s, q_r, peer, slot)
    grc = lambda peer, slot: copy_pw(gs, gr, gr_s, gr_r, peer, slot)
    lrc = lambda peer, slot: copy_pw(ls.at[peer], lr, ls_s, lr_r, peer, slot)

    def start_first(s):
        q = pw_peer(p, s)
        agp(q, p).start()
        agi(q, p).start()
        pjc(q, p).start()
    each(1, N_PW, start_first)
    each(1, N_BAND, lambda s: gbc(band_peer(s), b).start())

    def forward(s):
        blk = pw_peer(p, s)

        @pl.when(s > 0)
        def _():
            agp(blk, blk).wait_recv()
            agi(blk, blk).wait_recv()
        forward_block(ag_psi[blk], ag_idx[blk], p, blk, f_ref, v_ref, li_ref, acc_ref, CH)
    each(0, N_PW, forward)

    each(1, N_PW, lambda s: pjc(pw_peer(p, s), pw_peer(p, s)).wait_recv())
    proj = pj_recv[0]
    for k in range(1, N_PW):
        proj = proj + pj_recv[k]
    pr_ref[...] = proj
    dc = jnp.dot(proj, bd_ref[0], precision=lax.Precision.HIGHEST, preferred_element_type=F32)
    qc = jnp.dot(proj, bd_ref[1], precision=lax.Precision.HIGHEST, preferred_element_type=F32)
    q_send[...] = qc[0:2].astype(BF16).astype(F32)
    qb[b] = q_send[...]
    pad = jnp.zeros((4, 128), F32)
    left = jnp.concatenate([dc[0:2], qc[0:2], pad], axis=0).astype(BF16)[:, :72]
    right = jnp.concatenate([-dc[1:2], dc[0:1], -qc[1:2], qc[0:1], pad], axis=0).astype(BF16)[:, :72]
    nl_ref[...] = (jnp.dot(left, beta_ref[0], preferred_element_type=F32)
                   + jnp.dot(right, beta_ref[1], preferred_element_type=F32))
    s_out[...] = (psi_ref[...].astype(F32) + nl_ref[2:4, :]).astype(BF16)

    each(1, N_BAND, lambda s: gbc(band_peer(s), band_peer(s)).wait_recv())
    gre, gim = gb[:, 0, :].astype(BF16), gb[:, 1, :].astype(BF16)
    m_ref[:, 0, 0:48] = nt(gre, gre) + nt(gim, gim)
    m_ref[:, 1, 0:48] = nt(gre, gim) - nt(gim, gre)
    rb[b] = m_ref[b]

    each(0, KD, lambda j: dense_plane(j, f_ref, vloc_ref, zp, zm, xp, xm))

    def start_rows(s):
        rbc(band_peer(s), b).start()
        qbc(band_peer(s), b).start()
    each(1, N_BAND, start_rows)

    def backward(i):
        blk = pw_peer(p, 15 - i)

        @pl.when(i == 13)
        def _():
            each(1, N_BAND, lambda s: rbc(band_peer(s), band_peer(s)).wait_recv())
            tot = rb[0]
            for k in range(1, N_BAND):
                tot = tot + rb[k]
            gs[...] = tot
            gr[p] = tot
        re, im = backward_block(ag_idx[blk], p, blk, f_ref, e_ref, li_ref, b_ref, s_ref, CHB)
        loc_ref[0] = re
        loc_ref[1] = im
        ls[blk, 0] = re.astype(BF16)
        ls[blk, 1] = im.astype(BF16)

        @pl.when(i > 0)
        def _():
            prev = pw_peer(p, 16 - i)
            lrc(prev, p).start()

        @pl.when(i == 14)
        def _():
            each(1, N_PW, lambda s: grc(pw_peer(p, s), p).start())
    each(0, N_PW, backward)

    x, y, z = split_index(idx_ref[...])
    x = x + (p * KD).astype(F32)
    fold = lambda v: jnp.where(v < 96.0, v, v - 192.0)
    kin = 4.0 * (fold(x) * fold(x) + fold(y) * fold(y) + fold(z) * fold(z)) * (1.0 / (NG * NG))
    loc_ref[0] += kin * cf[:, 0, :]
    loc_ref[1] += kin * cf[:, 1, :]

    each(1, N_BAND, lambda s: qbc(band_peer(s), band_peer(s)).wait_recv())
    proj = pr_ref[...]
    hp = lax.Precision.HIGHEST
    u, w = nt(proj, qb[:, 0, :], precision=hp), nt(proj, qb[:, 1, :], precision=hp)
    corr = jnp.concatenate([u[0:1] + w[1:2], w[0:1] - u[1:2]], axis=0)
    each(1, N_PW, lambda s: grc(pw_peer(p, s), pw_peer(p, s)).wait_recv())
    tot = gr[0]
    for k in range(1, N_PW):
        tot = tot + gr[k]
    g_out[...] = (tot[:, 0:48] + corr) * (1.0 / 98304.0)

    def add_part(s):
        src = pw_peer(p, 16 - s)
        lrc(src, src).wait_recv()
        loc_ref[...] += lr[src].astype(F32)
    each(1, N_PW, add_part)
    for t in range(48):
        sl = slice(128 * t, 128 * (t + 1))
        h = jnp.concatenate([loc_ref[0, t:t + 1, :], loc_ref[1, t:t + 1, :]], axis=0)
        h_ref[:, sl] = (h + nl_ref[0:2, sl]).astype(BF16)

    def drain_pw(s):
        q = pw_peer(p, s)
        for c in (agp, agi, pjc, grc, lrc):
            c(q, p).wait_send()
    each(1, N_PW, drain_pw)

    def drain_band(s):
        q = band_peer(s)
        for c in (gbc, rbc, qbc):
            c(q, b).wait_send()
    each(1, N_BAND, drain_band)


def on_device(psi, gvec_index, vloc, beta, dmat, qmat):
    rows = psi.reshape(2, 6144)
    idx = gvec_index.reshape(48, 128)
    planes = jnp.transpose(vloc, (1, 0, 2))
    mats = jnp.swapaxes(jnp.stack([dmat, qmat]), 2, 3)
    bd = sum(jnp.pad(mats[:, a], ((0, 0), (18 * a, 110 - 18 * a), (18 * a, 110 - 18 * a))) for a in range(4))
    tabs = [jnp.asarray(t) for t in dft_tables()]
    vm = pltpu.VMEM
    dma = pltpu.SemaphoreType.DMA
    full = pl.BlockSpec(memory_space=vm)
    h, s, g = pl.pallas_call(
        kernel,
        out_shape=(jax.ShapeDtypeStruct((2, 6144), BF16), jax.ShapeDtypeStruct((2, 6144), BF16),
                   jax.ShapeDtypeStruct((2, 48), F32)),
        in_specs=[full] * 9,
        out_specs=(full,) * 3,
        scratch_shapes=[
            vm((16, 24, 16, 256), F32), vm((48, 24, 128), F32), vm((48, 8, 128), F32), vm((216, 256), F32),
            vm((48, 48, 128), F32), vm((216, 256), F32), vm((2, 48, 8, 128), F32), vm((8, 6144), F32),
            vm((2, 48, 128), F32), vm((8, 128), F32),
            vm((16, 2, 48, 128), BF16), vm((16, 48, 128), jnp.int32), vm((8, 128), F32), vm((16, 8, 128), F32),
            vm((48, 2, 128), F32), vm((48, 2, 128), F32), vm((48, 2, 128), F32), vm((48, 2, 128), F32),
            vm((2, 128), F32), vm((48, 2, 128), F32), vm((2, 128), F32), vm((16, 2, 128), F32),
            vm((16, 2, 48, 128), BF16), vm((16, 2, 48, 128), BF16),
        ] + [dma((16,))] * 6 + [dma((48,))] * 6 + [dma((16,))] * 4,
        compiler_params=pltpu.CompilerParams(collective_id=0, has_side_effects=True,
                                             vmem_limit_bytes=48 * 1024 * 1024),
    )(rows, idx, planes, beta, bd, *tabs)
    return h[:, None, :], s[:, None, :], g[:, None, :]


def solution(mesh):
    in_specs = (P(None, "band", "pw"), P("pw"), P(None, "pw", None), P(None, None, "pw"), P(), P())
    out_specs = (P(None, "band", "pw"), P(None, "band", "pw"), P(None, "band", None))
    return jax.shard_map(
        on_device, mesh=mesh, in_specs=in_specs, out_specs=out_specs, check_vma=False
    )
```

```python
import numpy as np
import jax, jax.numpy as jnp
from jax import lax
from jax.experimental import pallas as pl
from jax.experimental.pallas import tpu as pltpu
from jax.sharding import PartitionSpec as P

NG = 192
KD = 12
F32, BF16 = jnp.float32, jnp.bfloat16
TWO_PI = 2.0 * np.pi
CH = 48
CHB = 48


def dft_tables():
    j = np.arange(NG)
    ang = (j[:, None] * j[None, :] % NG).astype(np.float32) * np.float32(TWO_PI / NG)
    fac = np.float32(1.0) / np.sqrt(np.float32(NG))
    c = np.cos(ang).astype(np.float32) * fac
    s = np.sin(ang).astype(np.float32) * fac
    def zt(sign):
        t = np.zeros((512, 512), np.float32)
        t[:NG, :NG] = c; t[256:256 + NG, 256:256 + NG] = c
        t[:NG, 256:256 + NG] = sign * s; t[256:256 + NG, :NG] = -sign * s
        return t
    pad = (np.arange(NG) // KD) * 16 + np.arange(NG) % KD
    def xt(sign):
        t = np.zeros((2 * NG, 512), np.float32)
        t[:NG, pad] = c; t[NG:, 256 + pad] = c
        t[:NG, 256 + pad] = -sign * s; t[NG:, pad] = sign * s
        return t
    b = lambda t: np.asarray(t, dtype=jnp.bfloat16)
    return b(zt(1.0)), b(zt(-1.0)), b(xt(1.0)), b(xt(1.0).T)


def mod_floor(v, m):
    return v - m * jnp.floor((v + 0.5) * (1.0 / m))


def turn(t):
    h = t * np.float32(np.pi)
    q = h * h
    s = h * (1.0 + q * (-1 / 6 + q * (1 / 120 + q * (-1 / 5040 + q * (1 / 362880 + q * (-1 / 39916800))))))
    c = 1.0 + q * (-1 / 2 + q * (1 / 24 + q * (-1 / 720 + q * (1 / 40320 + q * (-1 / 3628800 + q * (1 / 479001600))))))
    return 1.0 - 2.0 * s * s, 2.0 * s * c


def split_index(idx):
    v = idx.astype(F32)
    x = jnp.floor((v + 0.5) * (1.0 / (NG * NG)))
    r = v - x * (NG * NG)
    y = jnp.floor((r + 0.5) * (1.0 / NG))
    return x, y, r - y * NG


def phases(y, p):
    fac = np.float32(1.0) / np.sqrt(np.float32(NG))
    m = mod_floor(y * p.astype(F32), 16.0)
    ar, ai = turn(jnp.where(m > 8.0, m - 16.0, m) * (1.0 / 16.0))
    wr, wi = turn(jnp.where(y > 96.0, y - 192.0, y) * np.float32(1.0 / NG))
    ar, ai = ar * fac, ai * fac
    out = []
    for j in range(KD):
        out.append((ar, ai))
        if j < KD - 1:
            ar, ai = ar * wr - ai * wi, ar * wi + ai * wr
    return out


def prep_index(idx, p, li_ref):
    x, y, z = split_index(idx)
    w = x * NG + z
    hi = jnp.floor((w + 0.5) * (1.0 / 256.0))
    li_ref[0:48, :] = w - hi * 256.0
    li_ref[48:96, :] = hi
    return phases(y, p)


def one_hot(li_ref, t, n):
    rows = lax.broadcasted_iota(jnp.int32, (256, 128), 0).astype(F32).astype(BF16)
    parts = []
    for k in range(n):
        lo = li_ref[t + k:t + k + 1, :].astype(BF16)
        parts.append(jnp.where(rows == lo, jnp.array(1, BF16), jnp.array(0, BF16)))
    return jnp.concatenate(parts, axis=1) if n > 1 else parts[0]


def spread(v_ref, li_ref, t, n):
    upper = (lax.broadcasted_iota(jnp.int32, (48, 128), 0) >= 24).astype(F32)
    cols = []
    for k in range(n):
        v = v_ref[24 * (t + k):24 * (t + k) + 24, :]
        v = jnp.concatenate([v, v], axis=0).astype(BF16)
        h = (li_ref[48 + t + k:49 + t + k, :] - upper).astype(BF16)
        zero = jnp.zeros_like(v)
        rows = [jnp.where(h == jnp.array(2 * q, BF16), v, zero) for q in range(4)]
        rows.append(jnp.where(h == jnp.array(8, BF16), v, zero)[:24])
        cols.append(jnp.concatenate(rows, axis=0))
    return jnp.concatenate(cols, axis=1) if n > 1 else cols[0]


def forward_block(psi, idx, p, base, f_ref, v_ref, li_ref, acc_ref, ch):
    e = prep_index(idx, p, li_ref)
    pr, pi = psi[0].astype(F32), psi[1].astype(F32)
    for j in range(KD):
        er, ei = e[j]
        v_ref[pl.ds(j, 48, stride=24), :] = pr * er - pi * ei
        v_ref[pl.ds(KD + j, 48, stride=24), :] = pr * ei + pi * er
    acc_ref[...] = jnp.zeros_like(acc_ref)

    def step(i, carry):
        t = i * ch
        zt = one_hot(li_ref, t, ch)
        l = spread(v_ref, li_ref, t, ch)
        acc_ref[...] += lax.dot_general(l, zt, (((1,), (1,)), ((), ())), preferred_element_type=F32)
        return carry
    if ch == 48:
        step(0, 0)
    else:
        lax.fori_loop(0, 48 // ch, step, 0)
    left = lax.broadcasted_iota(jnp.int32, (24, 128), 1) < 64
    for g in range(3):
        a = [[acc_ref[(3 * g + h) * 24:(3 * g + h + 1) * 24, 128 * q:128 * (q + 1)] for q in range(2)] for h in range(3)]
        r01, r10 = pltpu.roll(a[0][1], 64, 1), pltpu.roll(a[1][0], 64, 1)
        r20, r21 = pltpu.roll(a[2][0], 64, 1), pltpu.roll(a[2][1], 64, 1)
        pieces = [(a[0][0], a[0][1]), (jnp.where(left, r01, r10), r10), (a[1][1], a[2][0]), (jnp.where(left, r20, r21), r21)]
        for k, (low, high) in enumerate(pieces):
            rows = pl.ds(base * 16 + 4 * g + k, 24, stride=256)
            f_ref[0, rows, :] = low
            f_ref[1, rows, :] = high
    for k in range(KD, 16):
        rows = pl.ds(base * 16 + k, 24, stride=256)
        f_ref[0, rows, :] = jnp.zeros((24, 128), F32)
        f_ref[1, rows, :] = jnp.zeros((24, 128), F32)


def dense_plane(j, f_ref, vloc_ref, zp, zm, xp, xm):
    dot = lambda a, b: jnp.dot(a, b, preferred_element_type=F32)
    rows = [pl.ds(pl.multiple_of((c * KD + j) * 256, 256), 256) for c in range(2)]
    y = jnp.concatenate([f_ref[q, rows[c], :].astype(BF16) for c in range(2) for q in range(2)], axis=1)
    y = dot(y, zp[...]).astype(BF16)
    y = jnp.concatenate([y[:, 0:NG], y[:, 256:256 + NG]], axis=0)
    s = dot(xp[...], y)
    v = vloc_ref[j]
    s = jnp.concatenate([s[:NG] * v, s[NG:] * v], axis=0).astype(BF16)
    s = dot(xm[...], s).astype(BF16)
    out = dot(s[:256], zm[0:NG, :]) + dot(s[256:], zm[256:256 + NG, :])
    for c in range(2):
        for q in range(2):
            f_ref[q, rows[c], :] = out[:, 128 * (2 * c + q):128 * (2 * c + q + 1)]


def backward_block(idx, p, base, f_ref, e_ref, li_ref, b_ref, s_ref, ch, middle=lambda: None):
    e = prep_index(idx, p, li_ref)
    for j in range(KD):
        er, ei = e[j]
        e_ref[pl.ds(j, 48, stride=48), :] = er
        e_ref[pl.ds(KD + j, 48, stride=48), :] = ei
        e_ref[pl.ds(2 * KD + j, 48, stride=48), :] = -ei
        e_ref[pl.ds(3 * KD + j, 48, stride=48), :] = er
    left = lax.broadcasted_iota(jnp.int32, (24, 128), 1) < 64
    for g in range(3):
        x = []
        for k in range(4):
            x.append([f_ref[q, pl.ds(base * 16 + 4 * g + k, 24, stride=256), :] for q in range(2)])
        r10, r11 = pltpu.roll(x[1][0], 64, 1), pltpu.roll(x[1][1], 64, 1)
        r30, r31 = pltpu.roll(x[3][0], 64, 1), pltpu.roll(x[3][1], 64, 1)
        pieces = [(x[0][0], jnp.where(left, x[0][1], r10)), (jnp.where(left, r10, r11), x[2][0]),
                  (jnp.where(left, x[2][1], r30), jnp.where(left, r30, r31))]
        for h, (low, high) in enumerate(pieces):
            r = (3 * g + h) * 24
            b_ref[r:r + 24, 0:128] = low
            b_ref[r:r + 24, 128:256] = high

    middle()
    bm = b_ref[...].astype(BF16)

    def step(i, carry):
        t = i * ch
        tt = jnp.dot(bm, one_hot(li_ref, t, ch), preferred_element_type=F32)
        for k in range(ch):
            hi = jnp.broadcast_to(li_ref[48 + t + k:49 + t + k, :], (24, 128))
            sel = tt[0:24, 128 * k:128 * (k + 1)]
            for h in range(1, 9):
                sel = jnp.where(hi == float(h), tt[24 * h:24 * (h + 1), 128 * k:128 * (k + 1)], sel)
            ev = e_ref[48 * (t + k):48 * (t + k) + 48, :]
            a, b = sel * ev[:24], sel * ev[24:]
            s_ref[8 * (t + k):8 * (t + k) + 8, :] = a[0:8] + a[8:16] + a[16:24]
            s_ref[384 + 8 * (t + k):392 + 8 * (t + k), :] = b[0:8] + b[8:16] + b[16:24]
        return carry
    if ch == 48:
        step(0, 0)
    else:
        lax.fori_loop(0, 48 // ch, step, 0)
    re, im = (s_ref[pl.ds(c, 48, stride=8), :] for c in (0, 384))
    for k in range(1, 8):
        re = re + s_ref[pl.ds(k, 48, stride=8), :]
        im = im + s_ref[pl.ds(384 + k, 48, stride=8), :]
    return re, im


N_BAND = 48
N_PW = 16


def pw_peer(p, s):
    k = lax.div(s, 2)
    dy = lax.div(k + 1, 2) * (2 * lax.rem(k, 2) - 1)
    y = lax.rem(lax.div(p, 2) + dy + 8, 8)
    return 2 * y + lax.rem(p + s, 2)


def kernel(psi_hbm, idx_hbm, vloc_hbm, beta_hbm, d_hbm, q_hbm, zp_hbm, zm_hbm, xp_hbm, xm_hbm, h_ref, s_out, g_out,
           psi_ref, idx_ref, vloc_ref, beta_ref, d_ref, q_ref, zp, zm, xp, xm, bd_ref, corr_ref, in_sem,
           f_ref, v_ref, li_ref, acc_ref, e_ref, b_ref, s_ref, nl_ref, loc_ref, pr_ref,
           ag_psi, ag_idx, pj_send, pj_recv, cf, gb, m_ref, rb, q_send, qb, gs, gr, ls, lr,
           agp_s, agp_r, agi_s, agi_r, pj_s, pj_r, gb_s, gb_r, rb_s, rb_r, q_s, q_r, gr_s, gr_r, ls_s, lr_r):
    p, b = lax.axis_index("pw"), lax.axis_index("band")

    def band_peer(s):
        return lax.rem(b + s, N_BAND)

    def copy_pw(src, dst, ssem, rsem, peer, slot):
        return pltpu.make_async_remote_copy(src_ref=src, dst_ref=dst.at[slot], send_sem=ssem.at[peer],
                                            recv_sem=rsem.at[slot], device_id={"pw": peer},
                                            device_id_type=pl.DeviceIdType.MESH)

    def copy_band(src, dst, ssem, rsem, peer, slot):
        return pltpu.make_async_remote_copy(src_ref=src, dst_ref=dst.at[slot], send_sem=ssem.at[peer],
                                            recv_sem=rsem.at[slot], device_id={"band": peer},
                                            device_id_type=pl.DeviceIdType.MESH)

    def each(first, last, body):
        def step(s, carry):
            body(s)
            return carry
        lax.fori_loop(first, last, step, 0)

    loads = [pltpu.make_async_copy(src, dst, in_sem.at[k]) for k, (src, dst) in enumerate((
        (psi_hbm, psi_ref), (idx_hbm, idx_ref), (beta_hbm, beta_ref), (d_hbm, d_ref), (q_hbm, q_ref),
        (vloc_hbm, vloc_ref), (zp_hbm, zp), (zm_hbm, zm), (xp_hbm, xp), (xm_hbm, xm)))]
    for load in loads:
        load.start()
    barrier = pltpu.get_barrier_semaphore()
    each(1, N_PW, lambda s: pl.semaphore_signal(barrier, inc=1, device_id={"pw": pw_peer(p, s)},
                                                device_id_type=pl.DeviceIdType.MESH))
    each(1, N_BAND, lambda s: pl.semaphore_signal(barrier, inc=1, device_id={"band": band_peer(s)},
                                                  device_id_type=pl.DeviceIdType.MESH))

    loads[0].wait()
    loads[1].wait()
    for t in range(48):
        cf[t] = psi_ref[:, 128 * t:128 * (t + 1)].astype(F32)
    ag_psi[p, 0] = cf[:, 0, :].astype(BF16)
    ag_psi[p, 1] = cf[:, 1, :].astype(BF16)
    ag_idx[p] = idx_ref[...]
    gb[b] = cf[b]
    nt = lambda u, w, **k: lax.dot_general(u, w, (((1,), (1,)), ((), ())), preferred_element_type=F32, **k)
    agp = lambda peer, slot: copy_pw(ag_psi.at[p], ag_psi, agp_s, agp_r, peer, slot)
    agi = lambda peer, slot: copy_pw(ag_idx.at[p], ag_idx, agi_s, agi_r, peer, slot)
    pjc = lambda peer, slot: copy_pw(pj_send, pj_recv, pj_s, pj_r, peer, slot)
    gbc = lambda peer, slot: copy_band(cf.at[peer], gb, gb_s, gb_r, peer, slot)
    rbc = lambda peer, slot: copy_band(m_ref.at[peer], rb, rb_s, rb_r, peer, slot)
    qbc = lambda peer, slot: copy_band(q_send, qb, q_s, q_r, peer, slot)
    grc = lambda peer, slot: copy_pw(gs, gr, gr_s, gr_r, peer, slot)
    lrc = lambda peer, slot: copy_pw(ls.at[peer], lr, ls_s, lr_r, peer, slot)

    loads[2].wait()
    rows = psi_ref[...]
    pr, pi = nt(rows, beta_ref[0]), nt(rows, beta_ref[1])
    pj_send[...] = jnp.zeros_like(pj_send)
    pj_send[0:1, 0:72] = pr[0:1] + pi[1:2]
    pj_send[1:2, 0:72] = pr[1:2] - pi[0:1]
    pj_recv[p] = pj_send[...]
    m_ref[...] = jnp.zeros_like(m_ref)
    partner = pw_peer(p, 1)

    def start_first(s):
        q = pw_peer(p, s)
        pjc(q, p).start()

        @pl.when(jnp.logical_or(s == 1, lax.rem(s, 2) == 0))
        def _():
            agp(q, p).start()
            agi(q, p).start()

    def pass_on(blk):
        slot = 2 * lax.div(blk, 2) + 1 - lax.rem(blk, 2)
        return [pltpu.make_async_remote_copy(src_ref=buf.at[blk], dst_ref=buf.at[blk], send_sem=ssem.at[slot],
                                             recv_sem=rsem.at[blk], device_id={"pw": partner},
                                             device_id_type=pl.DeviceIdType.MESH)
                for buf, ssem, rsem in ((ag_psi, agp_s, agp_r), (ag_idx, agi_s, agi_r))]

    def forward(s):
        blk = pw_peer(p, s)
        forward_block(ag_psi[blk], ag_idx[blk], p, blk, f_ref, v_ref, li_ref, acc_ref, CH)

        @pl.when(s == 0)
        def _():
            pl.semaphore_wait(barrier, N_PW + N_BAND - 2)
            each(1, N_PW, start_first)
            each(1, N_BAND, lambda s: gbc(band_peer(s), b).start())

        @pl.when(s < N_PW - 1)
        def _():
            new = pw_peer(p, s + 1)
            agp(new, new).wait_recv()
            agi(new, new).wait_recv()

        @pl.when(jnp.logical_and(s < N_PW - 1, lax.rem(s, 2) == 1))
        def _():
            for copy in pass_on(pw_peer(p, s + 1)):
                copy.start()
    each(0, N_PW, forward)

    each(1, N_PW, lambda s: pjc(pw_peer(p, s), pw_peer(p, s)).wait_recv())
    proj = pj_recv[0]
    for k in range(1, N_PW):
        proj = proj + pj_recv[k]
    pr_ref[...] = proj
    for k in range(3, 10):
        loads[k].wait()
    bd_ref[...] = jnp.zeros_like(bd_ref)
    for a in range(4):
        sl = slice(18 * a, 18 * a + 18)
        bd_ref[0, sl, sl] = d_ref[:, a, :]
        bd_ref[1, sl, sl] = q_ref[:, a, :]
    dc = nt(proj, bd_ref[0], precision=lax.Precision.HIGHEST)
    qc = nt(proj, bd_ref[1], precision=lax.Precision.HIGHEST)
    q_send[...] = qc[0:2].astype(BF16).astype(F32)
    qb[b] = q_send[...]
    pad = jnp.zeros((4, 128), F32)
    left = jnp.concatenate([dc[0:2], qc[0:2], pad], axis=0).astype(BF16)[:, :72]
    right = jnp.concatenate([-dc[1:2], dc[0:1], -qc[1:2], qc[0:1], pad], axis=0).astype(BF16)[:, :72]
    nl_ref[...] = (jnp.dot(left, beta_ref[0], preferred_element_type=F32)
                   + jnp.dot(right, beta_ref[1], preferred_element_type=F32))
    s_out[...] = (psi_ref[...].astype(F32) + nl_ref[2:4, :]).astype(BF16)

    each(1, N_BAND, lambda s: gbc(band_peer(s), band_peer(s)).wait_recv())
    gre, gim = gb[:, 0, :].astype(BF16), gb[:, 1, :].astype(BF16)
    m_ref[:, 0, 0:48] = nt(gre, gre) + nt(gim, gim)
    m_ref[:, 1, 0:48] = nt(gre, gim) - nt(gim, gre)
    rb[b] = m_ref[b]

    def dense(j):
        dense_plane(2 * j, f_ref, vloc_ref, zp, zm, xp, xm)
        dense_plane(2 * j + 1, f_ref, vloc_ref, zp, zm, xp, xm)
    each(0, KD // 2, dense)

    def start_rows(s):
        rbc(band_peer(s), b).start()
        qbc(band_peer(s), b).start()
    each(1, N_BAND, start_rows)

    def backward(i):
        blk = pw_peer(p, 15 - i)

        def middle():
            @pl.when(i > 0)
            def _():
                lrc(pw_peer(p, 16 - i), p).start()
        re, im = backward_block(ag_idx[blk], p, blk, f_ref, e_ref, li_ref, b_ref, s_ref, CHB, middle)
        loc_ref[0] = re
        loc_ref[1] = im
        ls[blk, 0] = re.astype(BF16)
        ls[blk, 1] = im.astype(BF16)

        @pl.when(i == 7)
        def _():
            each(1, N_BAND, lambda s: rbc(band_peer(s), band_peer(s)).wait_recv())
            each(1, N_BAND, lambda s: qbc(band_peer(s), band_peer(s)).wait_recv())
            tot = rb[0]
            for k in range(1, N_BAND):
                tot = tot + rb[k]
            gs[...] = tot
            gr[p] = tot
            proj = pr_ref[...]
            hp = lax.Precision.HIGHEST
            u, w = nt(proj, qb[:, 0, :], precision=hp), nt(proj, qb[:, 1, :], precision=hp)
            corr_ref[...] = jnp.concatenate([u[0:1] + w[1:2], w[0:1] - u[1:2]], axis=0)

        @pl.when(i == 8)
        def _():
            each(1, N_PW, lambda s: grc(pw_peer(p, s), p).start())
    each(0, N_PW, backward)

    x, y, z = split_index(idx_ref[...])
    x = x + (p * KD).astype(F32)
    fold = lambda v: jnp.where(v < 96.0, v, v - 192.0)
    kin = 4.0 * (fold(x) * fold(x) + fold(y) * fold(y) + fold(z) * fold(z)) * (1.0 / (NG * NG))
    loc_ref[0] += kin * cf[:, 0, :]
    loc_ref[1] += kin * cf[:, 1, :]

    each(1, N_PW, lambda s: grc(pw_peer(p, s), pw_peer(p, s)).wait_recv())
    tot = gr[0]
    for k in range(1, N_PW):
        tot = tot + gr[k]
    g_out[...] = (tot[:, 0:48] + corr_ref[...]) * (1.0 / 98304.0)

    def add_part(s):
        src = pw_peer(p, 16 - s)
        lrc(src, src).wait_recv()
        loc_ref[...] += lr[src].astype(F32)
    each(1, N_PW, add_part)
    for t in range(48):
        sl = slice(128 * t, 128 * (t + 1))
        h = jnp.concatenate([loc_ref[0, t:t + 1, :], loc_ref[1, t:t + 1, :]], axis=0)
        h_ref[:, sl] = (h + nl_ref[0:2, sl]).astype(BF16)

    def drain_pw(s):
        q = pw_peer(p, s)
        for c in (agp, agi, pjc, grc, lrc):
            c(q, p).wait_send()
    each(1, N_PW, drain_pw)

    def drain_band(s):
        q = band_peer(s)
        for c in (gbc, rbc, qbc):
            c(q, b).wait_send()
    each(1, N_BAND, drain_band)


def on_device(psi, gvec_index, vloc, beta, dmat, qmat):
    rows = psi.reshape(2, 6144)
    idx = gvec_index.reshape(48, 128)
    planes = jnp.transpose(vloc, (1, 0, 2))
    mats = [jnp.transpose(m, (1, 0, 2)) for m in (dmat, qmat)]
    tabs = [jnp.asarray(t) for t in dft_tables()]
    vm = pltpu.VMEM
    dma = pltpu.SemaphoreType.DMA
    full = pl.BlockSpec(memory_space=vm)
    h, s, g = pl.pallas_call(
        kernel,
        out_shape=(jax.ShapeDtypeStruct((2, 6144), BF16), jax.ShapeDtypeStruct((2, 6144), BF16),
                   jax.ShapeDtypeStruct((2, 48), F32)),
        in_specs=[pl.BlockSpec(memory_space=pl.ANY)] * 10,
        out_specs=(full,) * 3,
        scratch_shapes=[
            vm((2, 6144), BF16), vm((48, 128), jnp.int32), vm((KD, NG, NG), F32), vm((2, 72, 6144), BF16),
            vm((18, 4, 18), F32), vm((18, 4, 18), F32), vm((512, 512), BF16), vm((512, 512), BF16),
            vm((384, 512), BF16), vm((512, 384), BF16), vm((2, 128, 128), F32), vm((2, 48), F32), dma((10,)),
            vm((2, 6400, 128), F32), vm((1176, 128), F32), vm((96, 128), F32), vm((216, 256), F32),
            vm((2352, 128), F32), vm((216, 256), F32), vm((776, 128), F32), vm((8, 6144), F32),
            vm((2, 48, 128), F32), vm((8, 128), F32),
            vm((16, 2, 48, 128), BF16), vm((16, 48, 128), jnp.int32), vm((8, 128), F32), vm((16, 8, 128), F32),
            vm((48, 2, 128), F32), vm((48, 2, 128), F32), vm((48, 2, 128), F32), vm((48, 2, 128), F32),
            vm((2, 128), F32), vm((48, 2, 128), F32), vm((2, 128), F32), vm((16, 2, 128), F32),
            vm((16, 2, 48, 128), BF16), vm((16, 2, 48, 128), BF16),
        ] + [dma((16,))] * 6 + [dma((48,))] * 6 + [dma((16,))] * 4,
        compiler_params=pltpu.CompilerParams(collective_id=0, has_side_effects=True,
                                             vmem_limit_bytes=60 * 1024 * 1024),
    )(rows, idx, planes, beta, *mats, *tabs)
    return h[:, None, :], s[:, None, :], g[:, None, :]


def solution(mesh):
    in_specs = (P(None, "band", "pw"), P("pw"), P(None, "pw", None), P(None, None, "pw"), P(), P())
    out_specs = (P(None, "band", "pw"), P(None, "band", "pw"), P(None, "band", None))
    return jax.shard_map(
        on_device, mesh=mesh, in_specs=in_specs, out_specs=out_specs, check_vma=False
    )
```

```python
import numpy as np
import jax, jax.numpy as jnp
from jax import lax
from jax.experimental import pallas as pl
from jax.experimental.pallas import tpu as pltpu
from jax.sharding import PartitionSpec as P

NG = 192
KD = 12
F32, BF16 = jnp.float32, jnp.bfloat16
TWO_PI = 2.0 * np.pi
CH = 48
CHB = 48


def dft_tables():
    j = np.arange(NG)
    ang = (j[:, None] * j[None, :] % NG).astype(np.float32) * np.float32(TWO_PI / NG)
    fac = np.float32(1.0) / np.sqrt(np.float32(NG))
    c = np.cos(ang).astype(np.float32) * fac
    s = np.sin(ang).astype(np.float32) * fac
    def zt(sign):
        t = np.zeros((512, 512), np.float32)
        t[:NG, :NG] = c; t[256:256 + NG, 256:256 + NG] = c
        t[:NG, 256:256 + NG] = sign * s; t[256:256 + NG, :NG] = -sign * s
        return t
    pad = (np.arange(NG) // KD) * 16 + np.arange(NG) % KD
    def xt(sign):
        t = np.zeros((2 * NG, 512), np.float32)
        t[:NG, pad] = c; t[NG:, 256 + pad] = c
        t[:NG, 256 + pad] = -sign * s; t[NG:, pad] = sign * s
        return t
    b = lambda t: np.asarray(t, dtype=jnp.bfloat16)
    return b(zt(1.0)), b(zt(-1.0)), b(xt(1.0)), b(xt(1.0).T)


def mod_floor(v, m):
    return v - m * jnp.floor((v + 0.5) * (1.0 / m))


def turn(t):
    h = t * np.float32(np.pi)
    q = h * h
    s = h * (1.0 + q * (-1 / 6 + q * (1 / 120 + q * (-1 / 5040 + q * (1 / 362880 + q * (-1 / 39916800))))))
    c = 1.0 + q * (-1 / 2 + q * (1 / 24 + q * (-1 / 720 + q * (1 / 40320 + q * (-1 / 3628800 + q * (1 / 479001600))))))
    return 1.0 - 2.0 * s * s, 2.0 * s * c


def split_index(idx):
    v = idx.astype(F32)
    x = jnp.floor((v + 0.5) * (1.0 / (NG * NG)))
    r = v - x * (NG * NG)
    y = jnp.floor((r + 0.5) * (1.0 / NG))
    return x, y, r - y * NG


def phases(y, p):
    fac = np.float32(1.0) / np.sqrt(np.float32(NG))
    m = mod_floor(y * p.astype(F32), 16.0)
    ar, ai = turn(jnp.where(m > 8.0, m - 16.0, m) * (1.0 / 16.0))
    wr, wi = turn(jnp.where(y > 96.0, y - 192.0, y) * np.float32(1.0 / NG))
    ar, ai = ar * fac, ai * fac
    out = []
    for j in range(KD):
        out.append((ar, ai))
        if j < KD - 1:
            ar, ai = ar * wr - ai * wi, ar * wi + ai * wr
    return out


def prep_index(idx, p, li_ref):
    x, y, z = split_index(idx)
    w = x * NG + z
    hi = jnp.floor((w + 0.5) * (1.0 / 256.0))
    li_ref[0:48, :] = w - hi * 256.0
    li_ref[48:96, :] = hi
    return phases(y, p)


def one_hot(li_ref, t, n):
    rows = lax.broadcasted_iota(jnp.int32, (256, 128), 0).astype(F32).astype(BF16)
    parts = []
    for k in range(n):
        lo = li_ref[t + k:t + k + 1, :].astype(BF16)
        parts.append(jnp.where(rows == lo, jnp.array(1, BF16), jnp.array(0, BF16)))
    return jnp.concatenate(parts, axis=1) if n > 1 else parts[0]


def spread(v_ref, li_ref, t, n):
    upper = (lax.broadcasted_iota(jnp.int32, (48, 128), 0) >= 24).astype(F32)
    cols = []
    for k in range(n):
        v = v_ref[24 * (t + k):24 * (t + k) + 24, :]
        v = jnp.concatenate([v, v], axis=0).astype(BF16)
        h = (li_ref[48 + t + k:49 + t + k, :] - upper).astype(BF16)
        zero = jnp.zeros_like(v)
        rows = [jnp.where(h == jnp.array(2 * q, BF16), v, zero) for q in range(4)]
        rows.append(jnp.where(h == jnp.array(8, BF16), v, zero)[:24])
        cols.append(jnp.concatenate(rows, axis=0))
    return jnp.concatenate(cols, axis=1) if n > 1 else cols[0]


def forward_block(psi, idx, p, base, f_ref, v_ref, li_ref, acc_ref, ch):
    e = prep_index(idx, p, li_ref)
    pr, pi = psi[0].astype(F32), psi[1].astype(F32)
    for j in range(KD):
        er, ei = e[j]
        v_ref[pl.ds(j, 48, stride=24), :] = pr * er - pi * ei
        v_ref[pl.ds(KD + j, 48, stride=24), :] = pr * ei + pi * er
    acc_ref[...] = jnp.zeros_like(acc_ref)

    def step(i, carry):
        t = i * ch
        zt = one_hot(li_ref, t, ch)
        l = spread(v_ref, li_ref, t, ch)
        acc_ref[...] += lax.dot_general(l, zt, (((1,), (1,)), ((), ())), preferred_element_type=F32)
        return carry
    if ch == 48:
        step(0, 0)
    else:
        lax.fori_loop(0, 48 // ch, step, 0)
    left = lax.broadcasted_iota(jnp.int32, (24, 128), 1) < 64
    for g in range(3):
        a = [[acc_ref[(3 * g + h) * 24:(3 * g + h + 1) * 24, 128 * q:128 * (q + 1)] for q in range(2)] for h in range(3)]
        r01, r10 = pltpu.roll(a[0][1], 64, 1), pltpu.roll(a[1][0], 64, 1)
        r20, r21 = pltpu.roll(a[2][0], 64, 1), pltpu.roll(a[2][1], 64, 1)
        pieces = [(a[0][0], a[0][1]), (jnp.where(left, r01, r10), r10), (a[1][1], a[2][0]), (jnp.where(left, r20, r21), r21)]
        for k, (low, high) in enumerate(pieces):
            rows = pl.ds(base * 16 + 4 * g + k, 24, stride=256)
            f_ref[0, rows, :] = low
            f_ref[1, rows, :] = high
    for k in range(KD, 16):
        rows = pl.ds(base * 16 + k, 24, stride=256)
        f_ref[0, rows, :] = jnp.zeros((24, 128), F32)
        f_ref[1, rows, :] = jnp.zeros((24, 128), F32)


def dense_plane(j, f_ref, vloc_ref, zp, zm, xp, xm):
    dot = lambda a, b: jnp.dot(a, b, preferred_element_type=F32)
    rows = [pl.ds(pl.multiple_of((c * KD + j) * 256, 256), 256) for c in range(2)]
    y = jnp.concatenate([f_ref[q, rows[c], :].astype(BF16) for c in range(2) for q in range(2)], axis=1)
    y = dot(y, zp[...]).astype(BF16)
    y = jnp.concatenate([y[:, 0:NG], y[:, 256:256 + NG]], axis=0)
    s = dot(xp[...], y)
    v = vloc_ref[j]
    s = jnp.concatenate([s[:NG] * v, s[NG:] * v], axis=0).astype(BF16)
    s = dot(xm[...], s).astype(BF16)
    out = dot(s[:256], zm[0:NG, :]) + dot(s[256:], zm[256:256 + NG, :])
    for c in range(2):
        for q in range(2):
            f_ref[q, rows[c], :] = out[:, 128 * (2 * c + q):128 * (2 * c + q + 1)]


def backward_block(idx, p, base, f_ref, e_ref, li_ref, b_ref, s_ref, ch, middle=lambda: None):
    e = prep_index(idx, p, li_ref)
    for j in range(KD):
        er, ei = e[j]
        e_ref[pl.ds(j, 48, stride=48), :] = er
        e_ref[pl.ds(KD + j, 48, stride=48), :] = ei
        e_ref[pl.ds(2 * KD + j, 48, stride=48), :] = -ei
        e_ref[pl.ds(3 * KD + j, 48, stride=48), :] = er
    left = lax.broadcasted_iota(jnp.int32, (24, 128), 1) < 64
    for g in range(3):
        x = []
        for k in range(4):
            x.append([f_ref[q, pl.ds(base * 16 + 4 * g + k, 24, stride=256), :] for q in range(2)])
        r10, r11 = pltpu.roll(x[1][0], 64, 1), pltpu.roll(x[1][1], 64, 1)
        r30, r31 = pltpu.roll(x[3][0], 64, 1), pltpu.roll(x[3][1], 64, 1)
        pieces = [(x[0][0], jnp.where(left, x[0][1], r10)), (jnp.where(left, r10, r11), x[2][0]),
                  (jnp.where(left, x[2][1], r30), jnp.where(left, r30, r31))]
        for h, (low, high) in enumerate(pieces):
            r = (3 * g + h) * 24
            b_ref[r:r + 24, 0:128] = low
            b_ref[r:r + 24, 128:256] = high

    middle()
    bm = b_ref[...].astype(BF16)

    def step(i, carry):
        t = i * ch
        tt = jnp.dot(bm, one_hot(li_ref, t, ch), preferred_element_type=F32)
        for k in range(ch):
            hi = jnp.broadcast_to(li_ref[48 + t + k:49 + t + k, :], (24, 128))
            sel = tt[0:24, 128 * k:128 * (k + 1)]
            for h in range(1, 9):
                sel = jnp.where(hi == float(h), tt[24 * h:24 * (h + 1), 128 * k:128 * (k + 1)], sel)
            ev = e_ref[48 * (t + k):48 * (t + k) + 48, :]
            a, b = sel * ev[:24], sel * ev[24:]
            s_ref[8 * (t + k):8 * (t + k) + 8, :] = a[0:8] + a[8:16] + a[16:24]
            s_ref[384 + 8 * (t + k):392 + 8 * (t + k), :] = b[0:8] + b[8:16] + b[16:24]
        return carry
    if ch == 48:
        step(0, 0)
    else:
        lax.fori_loop(0, 48 // ch, step, 0)
    re, im = (s_ref[pl.ds(c, 48, stride=8), :] for c in (0, 384))
    for k in range(1, 8):
        re = re + s_ref[pl.ds(k, 48, stride=8), :]
        im = im + s_ref[pl.ds(384 + k, 48, stride=8), :]
    return re, im


N_BAND = 48
N_PW = 16


def pw_peer(p, s):
    k = lax.div(s, 2)
    dy = lax.div(k + 1, 2) * (2 * lax.rem(k, 2) - 1)
    y = lax.rem(lax.div(p, 2) + dy + 8, 8)
    return 2 * y + lax.rem(p + s, 2)


def kernel(psi_hbm, idx_hbm, vloc_hbm, beta_hbm, d_hbm, q_hbm, zp_hbm, zm_hbm, xp_hbm, xm_hbm, h_ref, s_out, g_out,
           psi_ref, idx_ref, vloc_ref, beta_ref, d_ref, q_ref, zp, zm, xp, xm, bd_ref, corr_ref, in_sem,
           f_ref, v_ref, li_ref, acc_ref, e_ref, b_ref, s_ref, nl_ref, loc_ref, pr_ref,
           ag_psi, ag_idx, pj_send, pj_recv, cf, gb, m_ref, rb, gs, gr, ls, lr,
           agp_r, agi_r, agp_s, agi_s, pj_s, pj_r, gb_s, gb_r, rb_s, rb_r, gr_s, gr_r, ls_s, lr_r):
    p, b = lax.axis_index("pw"), lax.axis_index("band")

    def band_peer(s):
        return lax.rem(b + s, N_BAND)

    def copy(src, dst, ssem, rsem, **peer):
        return pltpu.make_async_remote_copy(src_ref=src, dst_ref=dst, send_sem=ssem, recv_sem=rsem,
                                            device_id=peer, device_id_type=pl.DeviceIdType.MESH)

    def each(first, last, body):
        def step(s, carry):
            body(s)
            return carry
        lax.fori_loop(first, last, step, 0)

    loads = [pltpu.make_async_copy(src, dst, in_sem.at[k]) for k, (src, dst) in enumerate((
        (psi_hbm, psi_ref), (idx_hbm, idx_ref), (beta_hbm, beta_ref), (d_hbm, d_ref), (q_hbm, q_ref),
        (vloc_hbm, vloc_ref), (zp_hbm, zp), (zm_hbm, zm), (xp_hbm, xp), (xm_hbm, xm)))]
    for load in loads:
        load.start()
    barrier = pltpu.get_barrier_semaphore()
    each(1, N_PW, lambda s: pl.semaphore_signal(barrier, inc=1, device_id={"pw": pw_peer(p, s)},
                                                device_id_type=pl.DeviceIdType.MESH))
    each(1, N_BAND, lambda s: pl.semaphore_signal(barrier, inc=1, device_id={"band": band_peer(s)},
                                                  device_id_type=pl.DeviceIdType.MESH))

    loads[0].wait()
    loads[1].wait()
    for t in range(48):
        cf[t] = psi_ref[:, 128 * t:128 * (t + 1)].astype(F32)
    ag_psi[p, 0] = cf[:, 0, :].astype(BF16)
    ag_psi[p, 1] = cf[:, 1, :].astype(BF16)
    ag_idx[p] = idx_ref[...]
    gb[b] = cf[b]
    nt = lambda u, w, **k: lax.dot_general(u, w, (((1,), (1,)), ((), ())), preferred_element_type=F32, **k)
    agp = lambda peer, slot: copy(ag_psi.at[p], ag_psi.at[slot], agp_s, agp_r.at[slot], pw=peer)
    agi = lambda peer, slot: copy(ag_idx.at[p], ag_idx.at[slot], agi_s, agi_r.at[slot], pw=peer)
    partner = pw_peer(p, 1)

    def all_of(buf, n, ssem, rsem):
        return copy(buf.at[pl.ds(0, n)], buf.at[pl.ds(0, n)], ssem, rsem, pw=partner)
    pj_all = all_of(pj_recv, N_PW - 1, pj_s, pj_r)
    gb_all = all_of(gb, N_BAND - 1, gb_s, gb_r)
    rb_all = all_of(rb, N_BAND - 1, rb_s, rb_r)
    gr_all = all_of(gr, N_PW - 1, gr_s, gr_r)
    lr_all = all_of(lr, N_PW - 1, ls_s, lr_r)

    loads[2].wait()
    rows = psi_ref[...]
    pr, pi = nt(rows, beta_ref[0]), nt(rows, beta_ref[1])
    pj_send[...] = jnp.zeros_like(pj_send)
    pj_send[0:1, 0:72] = pr[0:1] + pi[1:2]
    pj_send[1:2, 0:72] = pr[1:2] - pi[0:1]
    pj_recv[p] = pj_send[...]
    m_ref[...] = jnp.zeros_like(m_ref)

    def start_first(s):
        q = pw_peer(p, s)
        agp(q, p).start()
        agi(q, p).start()

    def start_proj(s):
        copy(pj_send, pj_recv.at[p], pj_s, pj_r, pw=pw_peer(p, s)).start()

    def start_chunk(s):
        q = band_peer(s)
        copy(cf.at[q], gb.at[b], gb_s, gb_r, band=q).start()

    def pass_on(blk):
        copy(ag_psi.at[blk], ag_psi.at[blk], agp_s, agp_r.at[blk], pw=partner).start()
        copy(ag_idx.at[blk], ag_idx.at[blk], agi_s, agi_r.at[blk], pw=partner).start()

    def forward(s):
        blk = pw_peer(p, s)
        forward_block(ag_psi[blk], ag_idx[blk], p, blk, f_ref, v_ref, li_ref, acc_ref, CH)

        @pl.when(s == 0)
        def _():
            pl.semaphore_wait(barrier, N_PW + N_BAND - 2)
            start_first(1)
            each(1, N_PW // 2, lambda k: start_first(2 * k))
            each(1, N_PW, start_proj)
            each(1, N_BAND, start_chunk)

        @pl.when(s < N_PW - 1)
        def _():
            new = pw_peer(p, s + 1)
            agp(new, new).wait_recv()
            agi(new, new).wait_recv()

        @pl.when(jnp.logical_and(s < N_PW - 1, lax.rem(s, 2) == 1))
        def _():
            pass_on(pw_peer(p, s + 1))
    each(0, N_PW, forward)

    pj_all.wait_recv()
    proj = pj_recv[0]
    for k in range(1, N_PW):
        proj = proj + pj_recv[k]
    pr_ref[...] = proj
    for k in range(3, 10):
        loads[k].wait()
    bd_ref[...] = jnp.zeros_like(bd_ref)
    for a in range(4):
        sl = slice(18 * a, 18 * a + 18)
        bd_ref[0, sl, sl] = d_ref[:, a, :]
        bd_ref[1, sl, sl] = q_ref[:, a, :]
    dc = nt(proj, bd_ref[0], precision=lax.Precision.HIGHEST)
    qc = nt(proj, bd_ref[1], precision=lax.Precision.HIGHEST)
    qc = qc.astype(BF16).astype(F32)
    m_ref[:, 2, :] = jnp.broadcast_to(qc[0:1], (48, 128))
    m_ref[:, 3, :] = jnp.broadcast_to(qc[1:2], (48, 128))
    pad = jnp.zeros((4, 128), F32)
    left = jnp.concatenate([dc[0:2], qc[0:2], pad], axis=0).astype(BF16)[:, :72]
    right = jnp.concatenate([-dc[1:2], dc[0:1], -qc[1:2], qc[0:1], pad], axis=0).astype(BF16)[:, :72]
    nl_ref[...] = (jnp.dot(left, beta_ref[0], preferred_element_type=F32)
                   + jnp.dot(right, beta_ref[1], preferred_element_type=F32))
    s_out[...] = psi_ref[...].astype(F32) + nl_ref[2:4, :]

    gb_all.wait_recv()
    gre, gim = gb[:, 0, :].astype(BF16), gb[:, 1, :].astype(BF16)
    m_ref[:, 0, 0:48] = nt(gre, gre) + nt(gim, gim)
    m_ref[:, 1, 0:48] = nt(gre, gim) - nt(gim, gre)
    rb[b] = m_ref[b]

    def dense(j):
        dense_plane(2 * j, f_ref, vloc_ref, zp, zm, xp, xm)
        dense_plane(2 * j + 1, f_ref, vloc_ref, zp, zm, xp, xm)
    each(0, KD // 2, dense)

    def start_rows(s):
        q = band_peer(s)
        copy(m_ref.at[q], rb.at[b], rb_s, rb_r, band=q).start()
    each(1, N_BAND, start_rows)

    def backward(i):
        blk = pw_peer(p, 15 - i)

        def middle():
            @pl.when(i > 0)
            def _():
                q = pw_peer(p, 16 - i)
                copy(ls.at[q], lr.at[p], ls_s, lr_r, pw=q).start()
        re, im = backward_block(ag_idx[blk], p, blk, f_ref, e_ref, li_ref, b_ref, s_ref, CHB, middle)
        loc_ref[0] = re
        loc_ref[1] = im
        ls[blk, 0] = re.astype(BF16)
        ls[blk, 1] = im.astype(BF16)

        @pl.when(i == 7)
        def _():
            rb_all.wait_recv()
            tot = rb[0]
            for k in range(1, N_BAND):
                tot = tot + rb[k]
            gs[...] = tot[0:2]
            gr[p] = tot[0:2]
            proj = pr_ref[...]
            hp = lax.Precision.HIGHEST
            u, w = nt(proj, rb[:, 2, :], precision=hp), nt(proj, rb[:, 3, :], precision=hp)
            corr_ref[...] = jnp.concatenate([u[0:1] + w[1:2], w[0:1] - u[1:2]], axis=0)

        @pl.when(i == 8)
        def _():
            each(1, N_PW, lambda s: copy(gs, gr.at[p], gr_s, gr_r, pw=pw_peer(p, s)).start())
    each(0, N_PW, backward)

    x, y, z = split_index(idx_ref[...])
    x = x + (p * KD).astype(F32)
    fold = lambda v: jnp.where(v < 96.0, v, v - 192.0)
    kin = 4.0 * (fold(x) * fold(x) + fold(y) * fold(y) + fold(z) * fold(z)) * (1.0 / (NG * NG))
    loc_ref[0] += kin * cf[:, 0, :]
    loc_ref[1] += kin * cf[:, 1, :]

    gr_all.wait_recv()
    tot = gr[0]
    for k in range(1, N_PW):
        tot = tot + gr[k]
    g_out[...] = tot[:, 0:48] + corr_ref[...]

    lr_all.wait_recv()

    def add_part(s):
        loc_ref[...] += lr[pw_peer(p, s)].astype(F32)
    each(1, N_PW, add_part)
    for t in range(48):
        sl = slice(128 * t, 128 * (t + 1))
        h = jnp.concatenate([loc_ref[0, t:t + 1, :], loc_ref[1, t:t + 1, :]], axis=0)
        h_ref[:, sl] = h + nl_ref[0:2, sl]

    for sent in (all_of(ag_psi, N_PW - 1, agp_s, agp_r.at[0]), all_of(ag_idx, N_PW - 1, agi_s, agi_r.at[0]),
                 pj_all, gb_all, rb_all, gr_all, lr_all):
        sent.wait_send()


def on_device(psi, gvec_index, vloc, beta, dmat, qmat):
    rows = psi.reshape(2, 6144)
    idx = gvec_index.reshape(48, 128)
    planes = jnp.transpose(vloc, (1, 0, 2))
    mats = [jnp.transpose(m, (1, 0, 2)) for m in (dmat, qmat)]
    tabs = [jnp.asarray(t) for t in dft_tables()]
    vm = pltpu.VMEM
    dma = pltpu.SemaphoreType.DMA
    full = pl.BlockSpec(memory_space=vm)
    h, s, g = pl.pallas_call(
        kernel,
        out_shape=(jax.ShapeDtypeStruct((2, 6144), F32),) * 2 + (jax.ShapeDtypeStruct((2, 48), F32),),
        in_specs=[pl.BlockSpec(memory_space=pl.ANY)] * 10,
        out_specs=(full,) * 3,
        scratch_shapes=[
            vm((2, 6144), BF16), vm((48, 128), jnp.int32), vm((KD, NG, NG), F32), vm((2, 72, 6144), BF16),
            vm((18, 4, 18), F32), vm((18, 4, 18), F32), vm((512, 512), BF16), vm((512, 512), BF16),
            vm((384, 512), BF16), vm((512, 384), BF16), vm((2, 128, 128), F32), vm((2, 48), F32), dma((10,)),
            vm((2, 6400, 128), F32), vm((1176, 128), F32), vm((96, 128), F32), vm((216, 256), F32),
            vm((2352, 128), F32), vm((216, 256), F32), vm((776, 128), F32), vm((8, 6144), F32),
            vm((2, 48, 128), F32), vm((8, 128), F32),
            vm((16, 2, 48, 128), BF16), vm((16, 48, 128), jnp.int32), vm((8, 128), F32), vm((16, 8, 128), F32),
            vm((48, 2, 128), F32), vm((48, 2, 128), F32), vm((48, 4, 128), F32), vm((48, 4, 128), F32),
            vm((2, 128), F32), vm((16, 2, 128), F32),
            vm((16, 2, 48, 128), BF16), vm((16, 2, 48, 128), BF16),
        ] + [dma((16,))] * 2 + [dma] * 12,
        compiler_params=pltpu.CompilerParams(collective_id=0, has_side_effects=True,
                                             vmem_limit_bytes=60 * 1024 * 1024),
    )(rows, idx, planes, beta, *mats, *tabs)
    h, s = h.astype(BF16), s.astype(BF16)
    return h[:, None, :], s[:, None, :], g[:, None, :] * (1.0 / 98304.0)


def solution(mesh):
    in_specs = (P(None, "band", "pw"), P("pw"), P(None, "pw", None), P(None, None, "pw"), P(), P())
    out_specs = (P(None, "band", "pw"), P(None, "band", "pw"), P(None, "band", None))
    return jax.shard_map(
        on_device, mesh=mesh, in_specs=in_specs, out_specs=out_specs, check_vma=False
    )
```

```python
import numpy as np
import jax, jax.numpy as jnp
from jax import lax
from jax.experimental import pallas as pl
from jax.experimental.pallas import tpu as pltpu
from jax.sharding import PartitionSpec as P

NG = 192
KD = 12
F32, BF16 = jnp.float32, jnp.bfloat16
TWO_PI = 2.0 * np.pi
CH = 48
CHB = 48


def dft_tables():
    j = np.arange(NG)
    ang = (j[:, None] * j[None, :] % NG).astype(np.float32) * np.float32(TWO_PI / NG)
    fac = np.float32(1.0) / np.sqrt(np.float32(NG))
    c = np.cos(ang).astype(np.float32) * fac
    s = np.sin(ang).astype(np.float32) * fac
    def zt(sign):
        t = np.zeros((512, 512), np.float32)
        t[:NG, :NG] = c; t[256:256 + NG, 256:256 + NG] = c
        t[:NG, 256:256 + NG] = sign * s; t[256:256 + NG, :NG] = -sign * s
        return t
    pad = (np.arange(NG) // KD) * 16 + np.arange(NG) % KD
    def xt(sign):
        t = np.zeros((2 * NG, 512), np.float32)
        t[:NG, pad] = c; t[NG:, 256 + pad] = c
        t[:NG, 256 + pad] = -sign * s; t[NG:, pad] = sign * s
        return t
    b = lambda t: np.asarray(t, dtype=jnp.bfloat16)
    return b(zt(1.0)), b(zt(-1.0)), b(xt(1.0)), b(xt(1.0).T)


def mod_floor(v, m):
    return v - m * jnp.floor((v + 0.5) * (1.0 / m))


def turn(t):
    h = t * np.float32(np.pi)
    q = h * h
    s = h * (1.0 + q * (-1 / 6 + q * (1 / 120 + q * (-1 / 5040 + q * (1 / 362880 + q * (-1 / 39916800))))))
    c = 1.0 + q * (-1 / 2 + q * (1 / 24 + q * (-1 / 720 + q * (1 / 40320 + q * (-1 / 3628800 + q * (1 / 479001600))))))
    return 1.0 - 2.0 * s * s, 2.0 * s * c


def split_index(idx):
    v = idx.astype(F32)
    x = jnp.floor((v + 0.5) * (1.0 / (NG * NG)))
    r = v - x * (NG * NG)
    y = jnp.floor((r + 0.5) * (1.0 / NG))
    return x, y, r - y * NG


def phases(y, p):
    fac = np.float32(1.0) / np.sqrt(np.float32(NG))
    m = mod_floor(y * p.astype(F32), 16.0)
    ar, ai = turn(jnp.where(m > 8.0, m - 16.0, m) * (1.0 / 16.0))
    wr, wi = turn(jnp.where(y > 96.0, y - 192.0, y) * np.float32(1.0 / NG))
    ar, ai = ar * fac, ai * fac
    out = []
    for j in range(KD):
        out.append((ar, ai))
        if j < KD - 1:
            ar, ai = ar * wr - ai * wi, ar * wi + ai * wr
    return out


def prep_index(idx, p, li_ref):
    x, y, z = split_index(idx)
    w = x * NG + z
    hi = jnp.floor((w + 0.5) * (1.0 / 256.0))
    li_ref[0:48, :] = w - hi * 256.0
    li_ref[48:96, :] = hi
    return phases(y, p)


def one_hot(li_ref, t, n):
    rows = lax.broadcasted_iota(jnp.int32, (256, 128), 0).astype(F32).astype(BF16)
    parts = []
    for k in range(n):
        lo = li_ref[t + k:t + k + 1, :].astype(BF16)
        parts.append(jnp.where(rows == lo, jnp.array(1, BF16), jnp.array(0, BF16)))
    return jnp.concatenate(parts, axis=1) if n > 1 else parts[0]


def spread(v_ref, li_ref, t, n):
    upper = (lax.broadcasted_iota(jnp.int32, (48, 128), 0) >= 24).astype(F32)
    cols = []
    for k in range(n):
        v = v_ref[24 * (t + k):24 * (t + k) + 24, :]
        v = jnp.concatenate([v, v], axis=0).astype(BF16)
        h = (li_ref[48 + t + k:49 + t + k, :] - upper).astype(BF16)
        zero = jnp.zeros_like(v)
        rows = [jnp.where(h == jnp.array(2 * q, BF16), v, zero) for q in range(4)]
        rows.append(jnp.where(h == jnp.array(8, BF16), v, zero)[:24])
        cols.append(jnp.concatenate(rows, axis=0))
    return jnp.concatenate(cols, axis=1) if n > 1 else cols[0]


def forward_block(psi, idx, p, base, f_ref, v_ref, li_ref, acc_ref, ch):
    e = prep_index(idx, p, li_ref)
    pr, pi = psi[0].astype(F32), psi[1].astype(F32)
    for j in range(KD):
        er, ei = e[j]
        v_ref[pl.ds(j, 48, stride=24), :] = pr * er - pi * ei
        v_ref[pl.ds(KD + j, 48, stride=24), :] = pr * ei + pi * er
    acc_ref[...] = jnp.zeros_like(acc_ref)

    def step(i, carry):
        t = i * ch
        zt = one_hot(li_ref, t, ch)
        l = spread(v_ref, li_ref, t, ch)
        acc_ref[...] += lax.dot_general(l, zt, (((1,), (1,)), ((), ())), preferred_element_type=F32)
        return carry
    if ch == 48:
        step(0, 0)
    else:
        lax.fori_loop(0, 48 // ch, step, 0)
    left = lax.broadcasted_iota(jnp.int32, (24, 128), 1) < 64
    for g in range(3):
        a = [[acc_ref[(3 * g + h) * 24:(3 * g + h + 1) * 24, 128 * q:128 * (q + 1)] for q in range(2)] for h in range(3)]
        r01, r10 = pltpu.roll(a[0][1], 64, 1), pltpu.roll(a[1][0], 64, 1)
        r20, r21 = pltpu.roll(a[2][0], 64, 1), pltpu.roll(a[2][1], 64, 1)
        pieces = [(a[0][0], a[0][1]), (jnp.where(left, r01, r10), r10), (a[1][1], a[2][0]), (jnp.where(left, r20, r21), r21)]
        for k, (low, high) in enumerate(pieces):
            rows = pl.ds(base * 16 + 4 * g + k, 24, stride=256)
            f_ref[0, rows, :] = low
            f_ref[1, rows, :] = high
    for k in range(KD, 16):
        rows = pl.ds(base * 16 + k, 24, stride=256)
        f_ref[0, rows, :] = jnp.zeros((24, 128), F32)
        f_ref[1, rows, :] = jnp.zeros((24, 128), F32)


def dense_plane(j, f_ref, vloc_ref, zp, zm, xp, xm):
    dot = lambda a, b: jnp.dot(a, b, preferred_element_type=F32)
    rows = [pl.ds(pl.multiple_of((c * KD + j) * 256, 256), 256) for c in range(2)]
    y = jnp.concatenate([f_ref[q, rows[c], :].astype(BF16) for c in range(2) for q in range(2)], axis=1)
    y = dot(y, zp[...]).astype(BF16)
    y = jnp.concatenate([y[:, 0:NG], y[:, 256:256 + NG]], axis=0)
    s = dot(xp[...], y)
    v = vloc_ref[j]
    s = jnp.concatenate([s[:NG] * v, s[NG:] * v], axis=0).astype(BF16)
    s = dot(xm[...], s).astype(BF16)
    out = dot(s[:256], zm[0:NG, :]) + dot(s[256:], zm[256:256 + NG, :])
    for c in range(2):
        for q in range(2):
            f_ref[q, rows[c], :] = out[:, 128 * (2 * c + q):128 * (2 * c + q + 1)]


def backward_block(idx, p, base, f_ref, e_ref, li_ref, b_ref, s_ref, ch, middle=lambda: None):
    e = prep_index(idx, p, li_ref)
    for j in range(KD):
        er, ei = e[j]
        e_ref[pl.ds(j, 48, stride=48), :] = er
        e_ref[pl.ds(KD + j, 48, stride=48), :] = ei
        e_ref[pl.ds(2 * KD + j, 48, stride=48), :] = -ei
        e_ref[pl.ds(3 * KD + j, 48, stride=48), :] = er
    left = lax.broadcasted_iota(jnp.int32, (24, 128), 1) < 64
    for g in range(3):
        x = []
        for k in range(4):
            x.append([f_ref[q, pl.ds(base * 16 + 4 * g + k, 24, stride=256), :] for q in range(2)])
        r10, r11 = pltpu.roll(x[1][0], 64, 1), pltpu.roll(x[1][1], 64, 1)
        r30, r31 = pltpu.roll(x[3][0], 64, 1), pltpu.roll(x[3][1], 64, 1)
        pieces = [(x[0][0], jnp.where(left, x[0][1], r10)), (jnp.where(left, r10, r11), x[2][0]),
                  (jnp.where(left, x[2][1], r30), jnp.where(left, r30, r31))]
        for h, (low, high) in enumerate(pieces):
            r = (3 * g + h) * 24
            b_ref[r:r + 24, 0:128] = low
            b_ref[r:r + 24, 128:256] = high

    middle()
    bm = b_ref[...].astype(BF16)

    def step(i, carry):
        t = i * ch
        tt = jnp.dot(bm, one_hot(li_ref, t, ch), preferred_element_type=F32)
        for k in range(ch):
            hi = jnp.broadcast_to(li_ref[48 + t + k:49 + t + k, :], (24, 128))
            sel = tt[0:24, 128 * k:128 * (k + 1)]
            for h in range(1, 9):
                sel = jnp.where(hi == float(h), tt[24 * h:24 * (h + 1), 128 * k:128 * (k + 1)], sel)
            ev = e_ref[48 * (t + k):48 * (t + k) + 48, :]
            a, b = sel * ev[:24], sel * ev[24:]
            s_ref[8 * (t + k):8 * (t + k) + 8, :] = a[0:8] + a[8:16] + a[16:24]
            s_ref[384 + 8 * (t + k):392 + 8 * (t + k), :] = b[0:8] + b[8:16] + b[16:24]
        return carry
    if ch == 48:
        step(0, 0)
    else:
        lax.fori_loop(0, 48 // ch, step, 0)
    re, im = (s_ref[pl.ds(c, 48, stride=8), :] for c in (0, 384))
    for k in range(1, 8):
        re = re + s_ref[pl.ds(k, 48, stride=8), :]
        im = im + s_ref[pl.ds(384 + k, 48, stride=8), :]
    return re, im


N_BAND = 48
N_PW = 16


def pw_peer(p, s):
    k = lax.div(s, 2)
    dy = lax.div(k + 1, 2) * (2 * lax.rem(k, 2) - 1)
    y = lax.rem(lax.div(p, 2) + dy + 8, 8)
    return 2 * y + lax.rem(p + s, 2)


def kernel(psi_hbm, idx_hbm, vloc_hbm, beta_hbm, d_hbm, q_hbm, zp_hbm, zm_hbm, xp_hbm, xm_hbm, h_ref, s_out, g_out,
           psi_ref, idx_ref, vloc_ref, beta_ref, d_ref, q_ref, zp, zm, xp, xm, bd_ref, corr_ref, in_sem,
           f_ref, v_ref, li_ref, acc_ref, e_ref, b_ref, s_ref, nl_ref, loc_ref, pr_ref,
           ag_psi, ag_idx, pj_send, pj_recv, cf, gb, m_ref, rb, gs, gr, ls, lr,
           agp_r, agi_r, agp_s, agi_s, pj_s, pj_r, gb_s, gb_r, rb_s, rb_r, gr_s, gr_r, ls_s, lr_r):
    p, b = lax.axis_index("pw"), lax.axis_index("band")

    def band_peer(s):
        return lax.rem(b + s, N_BAND)

    def copy(src, dst, ssem, rsem, **peer):
        return pltpu.make_async_remote_copy(src_ref=src, dst_ref=dst, send_sem=ssem, recv_sem=rsem,
                                            device_id=peer, device_id_type=pl.DeviceIdType.MESH)

    def each(first, last, body):
        def step(s, carry):
            body(s)
            return carry
        lax.fori_loop(first, last, step, 0)

    loads = [pltpu.make_async_copy(src, dst, in_sem.at[k]) for k, (src, dst) in enumerate((
        (psi_hbm, psi_ref), (idx_hbm, idx_ref), (beta_hbm, beta_ref), (d_hbm, d_ref), (q_hbm, q_ref),
        (vloc_hbm, vloc_ref), (zp_hbm, zp), (zm_hbm, zm), (xp_hbm, xp), (xm_hbm, xm)))]
    for load in loads[:3]:
        load.start()
    barrier = pltpu.get_barrier_semaphore()
    each(1, N_PW, lambda s: pl.semaphore_signal(barrier, inc=1, device_id={"pw": pw_peer(p, s)},
                                                device_id_type=pl.DeviceIdType.MESH))
    each(1, N_BAND, lambda s: pl.semaphore_signal(barrier, inc=1, device_id={"band": band_peer(s)},
                                                  device_id_type=pl.DeviceIdType.MESH))

    for load in loads[3:]:
        load.start()
    loads[0].wait()
    loads[1].wait()
    for t in range(48):
        cf[t] = psi_ref[:, 128 * t:128 * (t + 1)].astype(F32)
    ag_psi[p, 0] = cf[:, 0, :].astype(BF16)
    ag_psi[p, 1] = cf[:, 1, :].astype(BF16)
    ag_idx[p] = idx_ref[...]
    gb[b] = cf[b]
    nt = lambda u, w, **k: lax.dot_general(u, w, (((1,), (1,)), ((), ())), preferred_element_type=F32, **k)
    agp = lambda peer, slot: copy(ag_psi.at[p], ag_psi.at[slot], agp_s, agp_r.at[slot], pw=peer)
    agi = lambda peer, slot: copy(ag_idx.at[p], ag_idx.at[slot], agi_s, agi_r.at[slot], pw=peer)
    partner = pw_peer(p, 1)

    def all_of(buf, n, ssem, rsem):
        return copy(buf.at[pl.ds(0, n)], buf.at[pl.ds(0, n)], ssem, rsem, pw=partner)
    pj_all = all_of(pj_recv, N_PW - 1, pj_s, pj_r)
    gb_all = all_of(gb, N_BAND - 1, gb_s, gb_r)
    rb_all = all_of(rb, N_BAND - 1, rb_s, rb_r)
    gr_all = all_of(gr, N_PW - 1, gr_s, gr_r)
    lr_all = all_of(lr, N_PW - 1, ls_s, lr_r)

    loads[2].wait()
    rows = psi_ref[...]
    pr, pi = nt(rows, beta_ref[0]), nt(rows, beta_ref[1])
    pj_send[...] = jnp.zeros_like(pj_send)
    pj_send[0:1, 0:72] = pr[0:1] + pi[1:2]
    pj_send[1:2, 0:72] = pr[1:2] - pi[0:1]
    pj_recv[p] = pj_send[...]
    m_ref[...] = jnp.zeros_like(m_ref)
    for k in range(3, 5):
        loads[k].wait()
    bd_ref[...] = jnp.zeros_like(bd_ref)
    for a in range(4):
        sl = slice(18 * a, 18 * a + 18)
        bd_ref[0, sl, sl] = d_ref[:, a, :]
        bd_ref[1, sl, sl] = q_ref[:, a, :]

    def start_first(s):
        q = pw_peer(p, s)
        agp(q, p).start()
        agi(q, p).start()

    def start_proj(s):
        copy(pj_send, pj_recv.at[p], pj_s, pj_r, pw=pw_peer(p, s)).start()

    def start_chunk(s):
        q = band_peer(s)
        copy(cf.at[q], gb.at[b], gb_s, gb_r, band=q).start()

    def pass_on(blk):
        copy(ag_psi.at[blk], ag_psi.at[blk], agp_s, agp_r.at[blk], pw=partner).start()
        copy(ag_idx.at[blk], ag_idx.at[blk], agi_s, agi_r.at[blk], pw=partner).start()

    def forward(s):
        blk = pw_peer(p, s)
        forward_block(ag_psi[blk], ag_idx[blk], p, blk, f_ref, v_ref, li_ref, acc_ref, CH)

        @pl.when(s == 0)
        def _():
            pl.semaphore_wait(barrier, N_PW + N_BAND - 2)
            start_first(1)
            each(1, N_PW // 2, lambda k: start_first(2 * k))
            each(1, N_PW, start_proj)
            each(1, N_BAND, start_chunk)

        @pl.when(s < N_PW - 1)
        def _():
            new = pw_peer(p, s + 1)
            agp(new, new).wait_recv()
            agi(new, new).wait_recv()

        @pl.when(jnp.logical_and(s < N_PW - 1, lax.rem(s, 2) == 1))
        def _():
            pass_on(pw_peer(p, s + 1))
    each(0, N_PW, forward)

    pj_all.wait_recv()
    proj = pj_recv[0]
    for k in range(1, N_PW):
        proj = proj + pj_recv[k]
    pr_ref[...] = proj
    for k in range(5, 10):
        loads[k].wait()
    dc = nt(proj, bd_ref[0], precision=lax.Precision.HIGHEST)
    qc = nt(proj, bd_ref[1], precision=lax.Precision.HIGHEST)
    qc = qc.astype(BF16).astype(F32)
    m_ref[:, 2, :] = jnp.broadcast_to(qc[0:1], (48, 128))
    m_ref[:, 3, :] = jnp.broadcast_to(qc[1:2], (48, 128))
    pad = jnp.zeros((4, 128), F32)
    left = jnp.concatenate([dc[0:2], qc[0:2], pad], axis=0).astype(BF16)[:, :72]
    right = jnp.concatenate([-dc[1:2], dc[0:1], -qc[1:2], qc[0:1], pad], axis=0).astype(BF16)[:, :72]
    nl_ref[...] = (jnp.dot(left, beta_ref[0], preferred_element_type=F32)
                   + jnp.dot(right, beta_ref[1], preferred_element_type=F32))
    s_out[...] = psi_ref[...].astype(F32) + nl_ref[2:4, :]

    gb_all.wait_recv()
    gre, gim = gb[:, 0, :].astype(BF16), gb[:, 1, :].astype(BF16)
    m_ref[:, 0, 0:48] = nt(gre, gre) + nt(gim, gim)
    m_ref[:, 1, 0:48] = nt(gre, gim) - nt(gim, gre)
    rb[b] = m_ref[b]

    def dense(j):
        dense_plane(2 * j, f_ref, vloc_ref, zp, zm, xp, xm)
        dense_plane(2 * j + 1, f_ref, vloc_ref, zp, zm, xp, xm)
    each(0, KD // 2, dense)

    def start_rows(s):
        q = band_peer(s)
        copy(m_ref.at[q], rb.at[b], rb_s, rb_r, band=q).start()
    each(1, N_BAND, start_rows)

    def backward(i):
        blk = pw_peer(p, 15 - i)

        def middle():
            @pl.when(i > 0)
            def _():
                q = pw_peer(p, 16 - i)
                copy(ls.at[q], lr.at[p], ls_s, lr_r, pw=q).start()
        re, im = backward_block(ag_idx[blk], p, blk, f_ref, e_ref, li_ref, b_ref, s_ref, CHB, middle)
        loc_ref[0] = re
        loc_ref[1] = im
        ls[blk, 0] = re.astype(BF16)
        ls[blk, 1] = im.astype(BF16)

        @pl.when(i == 7)
        def _():
            rb_all.wait_recv()
            tot = rb[0]
            for k in range(1, N_BAND):
                tot = tot + rb[k]
            gs[...] = tot[0:2]
            gr[p] = tot[0:2]
            proj = pr_ref[...]
            hp = lax.Precision.HIGHEST
            u, w = nt(proj, rb[:, 2, :], precision=hp), nt(proj, rb[:, 3, :], precision=hp)
            corr_ref[...] = jnp.concatenate([u[0:1] + w[1:2], w[0:1] - u[1:2]], axis=0)

        @pl.when(i == 8)
        def _():
            each(1, N_PW, lambda s: copy(gs, gr.at[p], gr_s, gr_r, pw=pw_peer(p, s)).start())
    each(0, N_PW, backward)

    x, y, z = split_index(idx_ref[...])
    x = x + (p * KD).astype(F32)
    fold = lambda v: jnp.where(v < 96.0, v, v - 192.0)
    kin = 4.0 * (fold(x) * fold(x) + fold(y) * fold(y) + fold(z) * fold(z)) * (1.0 / (NG * NG))
    loc_ref[0] += kin * cf[:, 0, :]
    loc_ref[1] += kin * cf[:, 1, :]

    gr_all.wait_recv()
    tot = gr[0]
    for k in range(1, N_PW):
        tot = tot + gr[k]
    g_out[...] = tot[:, 0:48] + corr_ref[...]

    lr_all.wait_recv()

    def add_part(s):
        loc_ref[...] += lr[pw_peer(p, s)].astype(F32)
    each(1, N_PW, add_part)
    for t in range(48):
        sl = slice(128 * t, 128 * (t + 1))
        h = jnp.concatenate([loc_ref[0, t:t + 1, :], loc_ref[1, t:t + 1, :]], axis=0)
        h_ref[:, sl] = h + nl_ref[0:2, sl]

    for sent in (all_of(ag_psi, N_PW - 1, agp_s, agp_r.at[0]), all_of(ag_idx, N_PW - 1, agi_s, agi_r.at[0]),
                 pj_all, gb_all, rb_all, gr_all, lr_all):
        sent.wait_send()


def on_device(psi, gvec_index, vloc, beta, dmat, qmat):
    rows = psi.reshape(2, 6144)
    idx = gvec_index.reshape(48, 128)
    planes = jnp.transpose(vloc, (1, 0, 2))
    mats = [jnp.transpose(m, (1, 0, 2)) for m in (dmat, qmat)]
    tabs = [jnp.asarray(t) for t in dft_tables()]
    vm = pltpu.VMEM
    dma = pltpu.SemaphoreType.DMA
    full = pl.BlockSpec(memory_space=vm)
    h, s, g = pl.pallas_call(
        kernel,
        out_shape=(jax.ShapeDtypeStruct((2, 6144), F32),) * 2 + (jax.ShapeDtypeStruct((2, 48), F32),),
        in_specs=[pl.BlockSpec(memory_space=pl.ANY)] * 10,
        out_specs=(full,) * 3,
        scratch_shapes=[
            vm((2, 6144), BF16), vm((48, 128), jnp.int32), vm((KD, NG, NG), F32), vm((2, 72, 6144), BF16),
            vm((18, 4, 18), F32), vm((18, 4, 18), F32), vm((512, 512), BF16), vm((512, 512), BF16),
            vm((384, 512), BF16), vm((512, 384), BF16), vm((2, 128, 128), F32), vm((2, 48), F32), dma((10,)),
            vm((2, 6400, 128), F32), vm((1176, 128), F32), vm((96, 128), F32), vm((216, 256), F32),
            vm((2352, 128), F32), vm((216, 256), F32), vm((776, 128), F32), vm((8, 6144), F32),
            vm((2, 48, 128), F32), vm((8, 128), F32),
            vm((16, 2, 48, 128), BF16), vm((16, 48, 128), jnp.int32), vm((8, 128), F32), vm((16, 8, 128), F32),
            vm((48, 2, 128), F32), vm((48, 2, 128), F32), vm((48, 4, 128), F32), vm((48, 4, 128), F32),
            vm((2, 128), F32), vm((16, 2, 128), F32),
            vm((16, 2, 48, 128), BF16), vm((16, 2, 48, 128), BF16),
        ] + [dma((16,))] * 2 + [dma] * 12,
        compiler_params=pltpu.CompilerParams(collective_id=0, has_side_effects=True,
                                             vmem_limit_bytes=60 * 1024 * 1024),
    )(rows, idx, planes, beta, *mats, *tabs)
    h, s = h.astype(BF16), s.astype(BF16)
    return h[:, None, :], s[:, None, :], g[:, None, :] * (1.0 / 98304.0)


def solution(mesh):
    in_specs = (P(None, "band", "pw"), P("pw"), P(None, "pw", None), P(None, None, "pw"), P(), P())
    out_specs = (P(None, "band", "pw"), P(None, "band", "pw"), P(None, "band", None))
    return jax.shard_map(
        on_device, mesh=mesh, in_specs=in_specs, out_specs=out_specs, check_vma=False
    )
```
